512 devices in a mesh: ctx: 64 (over x, y, z_hi, core), head: 8 (over z_lo).
Axes of the slice: x: 4, y: 4, z: 16 (z_hi: 2, z_lo: 8; z = z_hi * 8 + z_lo), core: 2. Of those that a mesh axis runs over, the one named last changes fastest.
Arguments:
- queries: bfloat16 [8192, 8192], P('ctx', 'head'), parts along dimension 1, may hold values from -12 to 12
- key_rows: bfloat16 [8192, 1024], P('ctx', 'head'), parts along dimension 1, may hold values from -6 to 6
- value_rows: bfloat16 [8192, 1024], P('ctx', 'head'), parts along dimension 1, may hold values from -6 to 6
- out_grad: bfloat16 [8192, 8192], P('ctx', 'head'), parts along dimension 1, may hold values from -6 to 6
- doc_lengths: int32 [16], replicated, may hold values from 1 to 2048, 8192 in all
Outputs:
- attended: bfloat16 [8192, 8192], P('ctx', 'head'), parts along dimension 1
- query_grad: bfloat16 [8192, 8192], P('ctx', 'head'), parts along dimension 1
- key_grad: bfloat16 [8192, 1024], P('ctx', 'head'), parts along dimension 1
- value_grad: bfloat16 [8192, 1024], P('ctx', 'head'), parts along dimension 1
The draws below stay inside these ranges and needn't reach their ends.
There are 8 independent parts, one for each index of `head`. The reference program is written for one: setup_inputs(seed, part) draws one part's arguments, and reference() takes and returns one part's arrays. A program takes and returns all parts, laid end to end along the dimension named above; an argument that names none is the same for every part. Nothing has to cross between parts.
Inputs may be any that keep to these rules, and one draw needn't show every extreme that they name: `doc_lengths`: the documents lie end to end and cover all 8192 positions.
All inputs are finite; a program needn't handle non-finite values.
Results may differ from the reference program's by a relative error of at most 0.03.
Values may be sent and summed in bfloat16 or wider, within the bound.
A program may use at most 64 MiB of HBM per device.

```python
import math
import jax
import jax.numpy as jnp
import numpy as np
from jax import lax

GROUP = 8
HD = 128
TOKENS = 8192
DOC_MOST = 2048
NDOCS = 16


def draw_queries(key, part):
    drawn = jnp.clip(2.0 * jax.random.normal(jax.random.fold_in(key, 1), (TOKENS, GROUP * HD), jnp.float32), -12.0, 12.0)
    return drawn.astype(jnp.bfloat16)


def draw_key_rows(key, part):
    drawn = jnp.clip(jax.random.normal(jax.random.fold_in(key, 2), (TOKENS, HD), jnp.float32), -6.0, 6.0)
    return drawn.astype(jnp.bfloat16)


def steps_of(own_key, extent, split, least, top_value):
    loudness, own = 1.0, jax.random.fold_in(own_key, 6)
    for axis_at, parts in split:
        heights = jnp.exp(jax.random.uniform(jax.random.fold_in(own, axis_at), (parts,), jnp.float32, least / len(split), top_value / len(split)))
        loudness = loudness * jnp.repeat(heights, extent[axis_at] // parts).reshape([-1 if axis == axis_at else 1 for axis in range(len(extent))])
    return loudness


def length_profile(count, total, limit, slope):
    loads = [(1 << 20) // math.isqrt(grade ** slope) + 1 for grade in range(2, count + 1)]
    surplus, counts = total - limit - (count - 1), [1] * (count - 1)
    while surplus > 0:
        movable = [i for i in range(count - 1) if counts[i] < limit]
        pool, budget = sum([loads[i] for i in movable]), surplus
        for i in movable:
            more = min(limit - counts[i], max(1, budget * loads[i] // pool), surplus)
            counts[i] = counts[i] + more
            surplus = surplus - more
    return np.array([limit] + counts)


def ragged_sizes(own_key, count, total, limit, skew):
    if count == 2:
        one = jax.random.randint(own_key, (), max(1, total - limit), min(limit, total - 1) + 1)
        return jnp.stack([one, total - one])
    tallies = jnp.asarray(length_profile(count, total, limit, skew), jnp.int32)
    twos = (count - 1) // 2
    giver, sink = tallies[1:1 + 2 * twos:2], tallies[2:2 + 2 * twos:2]
    slack = jnp.minimum(giver - 1, limit - sink)
    moved = jax.random.randint(jax.random.fold_in(own_key, 1), (twos,), 0, 1 << 20) % (slack + 1)
    tallies = tallies.at[1:1 + 2 * twos:2].set(giver - moved).at[2:2 + 2 * twos:2].set(sink + moved)
    return tallies[jax.random.permutation(jax.random.fold_in(own_key, 2), count)]


def gaussian(own_key, extent, scale, most, shards=(), held_as=jnp.bfloat16):
    result = jax.random.normal(own_key, extent, jnp.float32) * scale
    if len(shards) > 0:
        result = steps_of(own_key, extent, shards, -0.22, 0.18) * result
    return jnp.clip(result, min=-most, max=most).astype(held_as)


def setup_inputs(seed: int = 0, part: int = 0) -> dict:
    streams_of = jax.random.split(jax.random.key(seed), 6)
    own_keys = jax.random.split(jax.random.fold_in(streams_of[5], part), 6)
    return {
        "queries": draw_queries(jax.random.fold_in(jax.random.fold_in(streams_of[5], part), 71), part),
        "key_rows": draw_key_rows(jax.random.fold_in(jax.random.fold_in(streams_of[5], part), 71), part),
        "value_rows": gaussian(own_keys[2], (TOKENS, HD), 1.0, 6.0, ((0, 64),)),
        "out_grad": gaussian(own_keys[3], (TOKENS, GROUP * HD), 1.0, 6.0, ((0, 64),)),
        "doc_lengths": ragged_sizes(streams_of[4], NDOCS, TOKENS, DOC_MOST, 2).astype(jnp.int32),
    }


big_negative = -1e30


def document_ids(doc_lengths, positions):
    doc_ends = jnp.cumsum(doc_lengths).astype(jnp.int32)
    doc_starts = doc_ends - doc_lengths
    passed = (positions[:, None] >= doc_starts[None, :]).astype(jnp.int32)
    return jnp.sum(passed, axis=1).astype(jnp.int32) - 1


def reference(queries, key_rows, value_rows, out_grad, doc_lengths):
    block_rows = min(512, TOKENS)
    block_count = TOKENS // block_rows
    span = DOC_MOST + block_rows
    score_scale = HD ** -0.5
    padding = jnp.zeros((DOC_MOST, HD), key_rows.dtype)
    keys_padded = jnp.concatenate([padding, key_rows], axis=0)
    values_padded = jnp.concatenate([padding, value_rows], axis=0)

    def one_block(carry, block_index):
        key_grads, value_grads = carry
        begin = (block_index * block_rows).astype(jnp.int32)
        query_pos = begin + jnp.arange(block_rows, dtype=jnp.int32)
        key_pos = begin - DOC_MOST + jnp.arange(span, dtype=jnp.int32)
        row_doc = jnp.repeat(document_ids(doc_lengths, query_pos), GROUP)
        row_pos = jnp.repeat(query_pos, GROUP)
        key_doc = document_ids(doc_lengths, key_pos)
        allowed = (row_doc[:, None] == key_doc[None, :]) & (row_pos[:, None] >= key_pos[None, :])
        query_block = lax.dynamic_slice_in_dim(queries, begin, block_rows, 0).reshape(block_rows * GROUP, HD)
        grad_block = lax.dynamic_slice_in_dim(out_grad, begin, block_rows, 0).reshape(block_rows * GROUP, HD)
        key_block = lax.dynamic_slice_in_dim(keys_padded, begin, span, 0)
        value_block = lax.dynamic_slice_in_dim(values_padded, begin, span, 0)
        scores = jnp.dot(query_block, key_block.T, preferred_element_type=jnp.float32) * score_scale
        masked = jnp.where(allowed, scores, big_negative)
        row_max = jnp.max(masked, axis=1)
        row_sum = jnp.sum(jnp.where(allowed, jnp.exp(masked - row_max[:, None]), 0.0), axis=1)
        log_total = row_max + jnp.log(row_sum)
        probability = jnp.where(allowed, jnp.exp(scores - log_total[:, None]), 0.0)
        rounded = probability.astype(jnp.bfloat16)
        attended = jnp.dot(rounded, value_block, preferred_element_type=jnp.float32).astype(jnp.bfloat16)
        row_delta = jnp.sum(grad_block.astype(jnp.float32) * attended.astype(jnp.float32), axis=1)
        prob_grad = jnp.dot(grad_block, value_block.T, preferred_element_type=jnp.float32)
        score_grad = (probability * (prob_grad - row_delta[:, None])).astype(jnp.bfloat16)
        query_grad = (jnp.dot(score_grad, key_block, preferred_element_type=jnp.float32) * score_scale).astype(jnp.bfloat16)
        key_part = jnp.dot(score_grad.T, query_block, preferred_element_type=jnp.float32) * score_scale
        value_part = jnp.dot(rounded.T, grad_block, preferred_element_type=jnp.float32)
        key_grads = lax.dynamic_update_slice_in_dim(key_grads, lax.dynamic_slice_in_dim(key_grads, begin, span, 0) + key_part, begin, 0)
        value_grads = lax.dynamic_update_slice_in_dim(value_grads, lax.dynamic_slice_in_dim(value_grads, begin, span, 0) + value_part, begin, 0)
        return (key_grads, value_grads), (attended.reshape(block_rows, GROUP * HD), query_grad.reshape(block_rows, GROUP * HD))

    initial = jnp.zeros((DOC_MOST + TOKENS, HD), jnp.float32)
    (key_grads, value_grads), (attended, query_grad) = lax.scan(one_block, (initial, initial), jnp.arange(block_count, dtype=jnp.int32))
    return (attended.reshape(TOKENS, GROUP * HD), query_grad.reshape(TOKENS, GROUP * HD),
            key_grads[DOC_MOST:].astype(jnp.bfloat16), value_grads[DOC_MOST:].astype(jnp.bfloat16))
```

```python
import functools
import math

import jax
import jax.numpy as jnp
from jax import lax
from jax.experimental import pallas as pl
from jax.experimental.pallas import tpu as pltpu
from jax.sharding import PartitionSpec as P

MESH = pl.DeviceIdType.MESH
T = 128
D = 128
G = 8
ROWS = T * G
PAIRS = 9
CHUNK = 256
NEG = -1e30
SCALE = D**-0.5
NT = (((1,), (1,)), ((), ()))
NN = (((1,), (0,)), ((), ()))
F32, BF16 = jnp.float32, jnp.bfloat16


def dot(a, b, dims):
    return lax.dot_general(a, b, dims, preferred_element_type=F32)


def kernel(
    n_ctx,
    q_hbm, k_hbm, v_hbm, g_hbm, lengths,
    att_hbm, dq_hbm, dk_hbm, dv_hbm,
    kv, qs, gs, qt, gt, sbuf, pbuf, bias, mrow, lrow, acc, att, dqo,
    part, s1, r1, s2, r2, r3, s3, r4, fin,
    ld_q, ld_g, ld_kv, st_att, st_dq, st_kv,
    z_s, own_s, rel_s, fwd_s, kr, fr, g1_s, g1_r, g2_s, g2_r, g3_r, g4_s, g4_r,
):
    c = lax.axis_index("ctx")
    z = lax.rem(c // 2, 2)
    core = lax.rem(c, 2)
    mate = c + 1 - 2 * core
    across = c + 2 - 4 * z
    low, high = pl.ds(0, T), pl.ds(T, T)

    def send(src, dst, ss, rs, dev):
        return pltpu.make_async_remote_copy(
            src_ref=src, dst_ref=dst, send_sem=ss, recv_sem=rs, device_id={"ctx": dev}, device_id_type=MESH
        )

    own_in = [
        pltpu.make_async_copy(src, kv.at[0, kind, low], ld_kv.at[kind]) for kind, src in enumerate((k_hbm, v_hbm))
    ]
    q_in = [
        pltpu.make_async_copy(q_hbm.at[:, pl.ds(h * D, D)], qs.at[pl.ds(h * T, T)], ld_q.at[h]) for h in range(G)
    ]
    g_in = [
        pltpu.make_async_copy(g_hbm.at[:, pl.ds(h * D, D)], gs.at[pl.ds(h * T, T)], ld_g.at[h]) for h in range(G)
    ]
    for copy in own_in + q_in + g_in:
        copy.start()

    def clear(i, _):
        kv[i] = jnp.zeros((2, 2 * T, D), BF16)
        return 0

    lax.fori_loop(1, PAIRS + 1, clear, 0)
    r2[...] = jnp.zeros_like(r2)
    r3[...] = jnp.zeros_like(r3)

    barrier = pltpu.get_barrier_semaphore()
    for dev in (mate, across):
        pl.semaphore_signal(barrier, inc=1, device_id={"ctx": dev}, device_id_type=MESH)
    count = 2
    for d in range(1, 5):
        up, down = c + 4 * d < n_ctx, c - 4 * d >= 0
        count = count + up.astype(jnp.int32) + down.astype(jnp.int32)

        @pl.when(up)
        def _():
            pl.semaphore_signal(barrier, inc=1, device_id={"ctx": c + 4 * d}, device_id_type=MESH)

        @pl.when(down)
        def _():
            pl.semaphore_signal(barrier, inc=1, device_id={"ctx": c - 4 * d}, device_id_type=MESH)

    for copy in own_in:
        copy.wait()
    pl.semaphore_wait(barrier, count)

    land = 1 + 8 * z
    here = 9 - 8 * z

    def z_send(kind):
        return send(kv.at[0, kind, low], kv.at[land, kind, low], z_s.at[kind], kr.at[land, kind], across)

    def own_send(d, kind):
        return send(
            kv.at[0, kind, low], kv.at[2 * d, kind, low], own_s.at[d, kind], kr.at[2 * d, kind], c + 4 * d
        )

    def relay_send(d, kind):
        to = 2 * d - 1 + 2 * z
        return send(kv.at[here, kind, low], kv.at[to, kind, low], rel_s.at[d, kind], kr.at[to, kind], c + 4 * d)

    def forward(i, kind):
        return send(kv.at[i, kind, low], kv.at[i, kind, high], fwd_s.at[i, kind], fr.at[i, kind], mate)

    def arrived(i, kind):
        return send(kv.at[i, kind, low], kv.at[i, kind, low], z_s.at[kind], kr.at[i, kind], mate)

    relays = lambda d: (c + 4 * d < n_ctx) & (2 * d - 1 + 2 * z < PAIRS)

    for kind in range(2):
        z_send(kind).start()
    for kind in range(2):
        forward(0, kind).start()
        for d in range(1, 5):

            @pl.when(c + 4 * d < n_ctx)
            def _():
                own_send(d, kind).start()

    row = c * T + lax.broadcasted_iota(jnp.int32, (T, 2 * T), 0)
    lane = lax.broadcasted_iota(jnp.int32, (T, 2 * T), 1)
    doc = jnp.zeros((T, 2 * T), jnp.int32)
    start = jnp.int32(0)
    for j in range(lengths.shape[0]):
        doc = jnp.where(row >= start, start, doc)
        start = start + lengths[j]
    first = lane + jnp.where(lane < T, c * T, mate * T - T)

    def mask(i, _):
        key = first - i * (2 * T)
        bias[i] = jnp.where((key >= doc) & (key <= row), 0.0, NEG)
        return 0

    lax.fori_loop(0, PAIRS, mask, 0)
    for copy in q_in:
        copy.wait()
    mrow[...] = jnp.full_like(mrow, NEG)

    def scores(i):
        key = kv[i, 0]
        b = bias[i]
        b = jnp.concatenate([b, b], axis=0)
        for t in range(ROWS // CHUNK):
            rows = pl.ds(t * CHUNK, CHUNK)
            s = dot(qs[rows], key, NT) + b
            sbuf[i, rows] = s
            mrow[rows] = jnp.maximum(mrow[rows], jnp.maximum(s[:, :T], s[:, T:]))

    def take(i, kind):
        @pl.when(c >= 2 * i)
        def _():
            arrived(i, kind).wait_recv()
            forward(i, kind).start()

    def near(n, _):
        i = 2 * n

        @pl.when(n < 4)
        def _():
            for kind in range(2):
                take(i + 2, kind)

        @pl.when(c >= 2 * i)
        def _():
            forward(i, 0).wait_recv()

        scores(i)
        return 0

    lax.fori_loop(0, 5, near, 0)

    for h in range(G):
        rows = pl.ds(h * T, T)
        qt[:, rows] = qs[rows].astype(F32).T.astype(BF16)

    for kind in range(2):
        arrived(here, kind).wait_recv()
        for d in range(1, 5):

            @pl.when(relays(d))
            def _():
                relay_send(d, kind).start()

    for kind in range(2):

        @pl.when(z == 1)
        def _():
            forward(1, kind).start()

        @pl.when(z == 0)
        def _():
            take(1, kind)

        for i in (3, 5, 7):
            take(i, kind)

    def far(n, _):
        i = 2 * n + 1

        @pl.when(c >= 2 * i)
        def _():
            forward(i, 0).wait_recv()

        scores(i)
        return 0

    lax.fori_loop(0, 4, far, 0)

    for t in range(ROWS // CHUNK):
        rows = pl.ds(t * CHUNK, CHUNK)
        mrow[rows] = jnp.broadcast_to(jnp.max(mrow[rows], axis=1, keepdims=True), (CHUNK, T))
    lrow[...] = jnp.zeros_like(lrow)
    acc[...] = jnp.zeros_like(acc)

    def weigh(n, _):
        i = jnp.where(n < 5, 2 * n, 2 * n - 9)

        @pl.when(c >= 2 * i)
        def _():
            forward(i, 1).wait_recv()

        value = kv[i, 1]
        for t in range(ROWS // CHUNK):
            rows = pl.ds(t * CHUNK, CHUNK)
            m = mrow[rows]
            p = jnp.exp2((sbuf[i, rows] - jnp.concatenate([m, m], axis=1)) * (SCALE * math.log2(math.e)))
            lrow[rows] += p[:, :T] + p[:, T:]
            p = p.astype(BF16)
            pbuf[i, rows] = p
            acc[rows] += dot(p, value, NN)
        return 0

    lax.fori_loop(0, PAIRS, weigh, 0)

    for copy in g_in:
        copy.wait()
    for h in range(G):
        rows = pl.ds(h * T, T)
        inverse = 1.0 / jnp.sum(lrow[rows], axis=1, keepdims=True)
        out = (acc[rows] * inverse).astype(BF16)
        att[rows] = out
        grad = (gs[rows].astype(F32) * inverse).astype(BF16)
        gs[rows] = grad
        grad = grad.astype(F32)
        gt[:, rows] = grad.T.astype(BF16)
        delta = jnp.sum(grad * out.astype(F32), axis=1, keepdims=True)
        lrow[rows] = jnp.broadcast_to(delta, (T, T))
    att_out = [
        pltpu.make_async_copy(att.at[pl.ds(h * T, T)], att_hbm.at[:, pl.ds(h * D, D)], st_att.at[h]) for h in range(G)
    ]
    for copy in att_out:
        copy.start()
    acc[...] = jnp.zeros_like(acc)

    def back(i):
        key, value = kv[i, 0], kv[i, 1]
        dk = jnp.zeros((D, 2 * T), F32)
        dv = jnp.zeros((D, 2 * T), F32)
        for t in range(ROWS // CHUNK):
            rows = pl.ds(t * CHUNK, CHUNK)
            p = pbuf[i, rows]
            delta = lrow[rows]
            ds = dot(gs[rows], value, NT) - jnp.concatenate([delta, delta], axis=1)
            ds = (p.astype(F32) * ds).astype(BF16)
            acc[rows] += dot(ds, key, NN)
            dk += dot(qt[:, rows], ds, NN)
            dv += dot(gt[:, rows], p, NN)
        part[i, 0] = dk[:, :T]
        part[i, 1] = dv[:, :T]
        s1[i, 0] = dk[:, T:].astype(BF16)
        s1[i, 1] = dv[:, T:].astype(BF16)

    def swap(i):
        return send(s1.at[i], r1.at[i], g1_s.at[i], g1_r.at[i], mate)

    def home(d):
        return send(s2.at[2 * d], r2.at[d], g2_s.at[2 * d], g2_r.at[d], c - 4 * d)

    def to_relay(i):
        d = (i + 1) // 2 - z
        return send(s2.at[i], r3.at[d], g2_s.at[i], g3_r.at[d], c - 4 * d)

    def back_across():
        return send(s3, r4, g4_s, g4_r, across)

    def child(d):
        return (c + 4 * d < n_ctx) & (2 * d - 1 + 2 * z < PAIRS)

    def order(n):
        return jnp.where(n < 4, 2 * n + 1, 16 - 2 * n)

    def pass_on(i):
        @pl.when(c >= 2 * i)
        def _():
            swap(i).wait_recv()
            total = part[i] + r1[i].astype(F32)
            part[i] = total
            s2[i] = total.astype(BF16)

            @pl.when(lax.rem(i, 2) == 0)
            def _():
                home(i // 2).start()

            @pl.when((lax.rem(i, 2) == 1) & ((z == 0) | (i > 1)))
            def _():
                to_relay(i).start()

    def backward(n, _):
        i = order(n)
        back(i)

        @pl.when(c >= 2 * i)
        def _():
            swap(i).start()

        @pl.when(n > 0)
        def _():
            pass_on(order(n - 1))

        @pl.when(n == 6)
        def _():
            for d in range(1, 5):

                @pl.when(child(d))
                def _():
                    send(s2.at[0], r3.at[d], g2_s.at[0], g3_r.at[d], mate).wait_recv()

            total = r3[1].astype(F32) + r3[2].astype(F32) + r3[3].astype(F32) + r3[4].astype(F32)
            total = total + part[1] * z.astype(F32)
            s3[...] = total.astype(BF16)
            back_across().start()

        return 0

    lax.fori_loop(0, PAIRS, backward, 0)

    for h in range(G):
        rows = pl.ds(h * T, T)
        dqo[rows] = (acc[rows] * SCALE).astype(BF16)
    dq_out = [
        pltpu.make_async_copy(dqo.at[pl.ds(h * T, T)], dq_hbm.at[:, pl.ds(h * D, D)], st_dq.at[h]) for h in range(G)
    ]
    for copy in dq_out:
        copy.start()

    swap(0).wait_recv()
    total = part[0] + r1[0].astype(F32)
    for d in range(1, 5):

        @pl.when(c + 4 * d < n_ctx)
        def _():
            send(s2.at[0], r2.at[d], g2_s.at[0], g2_r.at[d], mate).wait_recv()

    for d in range(1, 5):
        total = total + r2[d].astype(F32)
    back_across().wait_recv()
    total = total + r4[...].astype(F32)
    fin[0] = (total[0].T * SCALE).astype(BF16)
    fin[1] = total[1].T.astype(BF16)
    kv_out = [pltpu.make_async_copy(fin.at[j], ref, st_kv.at[j]) for j, ref in enumerate((dk_hbm, dv_hbm))]
    for copy in kv_out:
        copy.start()

    for kind in range(2):
        z_send(kind).wait_send()
        for d in range(1, 5):

            @pl.when(c + 4 * d < n_ctx)
            def _():
                own_send(d, kind).wait_send()

            @pl.when(relays(d))
            def _():
                relay_send(d, kind).wait_send()

        for i in range(PAIRS):

            @pl.when(c >= 2 * i)
            def _():
                forward(i, kind).wait_send()


    for i in range(PAIRS):

        @pl.when(c >= 2 * i)
        def _():
            swap(i).wait_send()
            if i > 0 and i % 2 == 0:
                home(i // 2).wait_send()
            if i > 1 and i % 2 == 1:
                to_relay(i).wait_send()

    @pl.when((z == 0) & (c >= 2))
    def _():
        to_relay(1).wait_send()

    back_across().wait_send()
    for copy in att_out + dq_out + kv_out:
        copy.wait()


def solution(mesh):
    n_ctx = mesh.shape["ctx"]

    def on_device(queries, key_rows, value_rows, out_grad, doc_lengths):
        anywhere = pl.BlockSpec(memory_space=pl.ANY)
        dma = pltpu.SemaphoreType.DMA
        vmem = pltpu.VMEM
        return pl.pallas_call(
            functools.partial(kernel, n_ctx),
            out_shape=(
                jax.ShapeDtypeStruct(queries.shape, BF16),
                jax.ShapeDtypeStruct(queries.shape, BF16),
                jax.ShapeDtypeStruct(key_rows.shape, BF16),
                jax.ShapeDtypeStruct(value_rows.shape, BF16),
            ),
            in_specs=[anywhere] * 4 + [pl.BlockSpec(memory_space=pltpu.SMEM)],
            out_specs=(anywhere,) * 4,
            scratch_shapes=[
                vmem((PAIRS + 1, 2, 2 * T, D), BF16),
                vmem((ROWS, D), BF16),
                vmem((ROWS, D), BF16),
                vmem((D, ROWS), BF16),
                vmem((D, ROWS), BF16),
                vmem((PAIRS, ROWS, 2 * T), F32),
                vmem((PAIRS, ROWS, 2 * T), BF16),
                vmem((PAIRS, T, 2 * T), F32),
                vmem((ROWS, T), F32),
                vmem((ROWS, T), F32),
                vmem((ROWS, D), F32),
                vmem((ROWS, D), BF16),
                vmem((ROWS, D), BF16),
                vmem((PAIRS, 2, D, T), F32),
                vmem((PAIRS, 2, D, T), BF16),
                vmem((PAIRS, 2, D, T), BF16),
                vmem((PAIRS, 2, D, T), BF16),
                vmem((5, 2, D, T), BF16),
                vmem((5, 2, D, T), BF16),
                vmem((2, D, T), BF16),
                vmem((2, D, T), BF16),
                vmem((2, T, D), BF16),
                dma((G,)), dma((G,)), dma((2,)), dma((G,)), dma((G,)), dma((2,)),
                dma((2,)), dma((5, 2)), dma((5, 2)), dma((PAIRS, 2)), dma((PAIRS + 1, 2)), dma((PAIRS, 2)),
                dma((PAIRS,)), dma((PAIRS,)), dma((PAIRS,)), dma((5,)), dma((5,)), dma, dma,
            ],
            compiler_params=pltpu.CompilerParams(
                collective_id=0, has_side_effects=True, vmem_limit_bytes=60 * 1024 * 1024
            ),
        )(queries, key_rows, value_rows, out_grad, doc_lengths)

    split = P("ctx", "head")
    return jax.shard_map(
        on_device, mesh=mesh, in_specs=(split, split, split, split, P()), out_specs=(split,) * 4, check_vma=False
    )
```

```python
import functools
import math

import jax
import jax.numpy as jnp
from jax import lax
from jax.experimental import pallas as pl
from jax.experimental.pallas import tpu as pltpu
from jax.sharding import PartitionSpec as P

MESH = pl.DeviceIdType.MESH
T = 128
D = 128
G = 8
ROWS = T * G
PAIRS = 9
CHUNK = 256
NEG = -1e30
SCALE = D**-0.5
LOG2 = SCALE * math.log2(math.e)
NT = (((1,), (1,)), ((), ()))
NN = (((1,), (0,)), ((), ()))
F32, BF16 = jnp.float32, jnp.bfloat16


def dot(a, b, dims):
    return lax.dot_general(a, b, dims, preferred_element_type=F32)


def kernel(
    n_ctx,
    q_hbm, k_hbm, v_hbm, g_hbm, lengths,
    att_hbm, dq_hbm, dk_hbm, dv_hbm,
    kv, qs, gs, g2, qt, gt, sbuf, pbuf, dsb, bias, m1, m2, l1, l2, acc, att, dqo,
    part, s1, r1, s2, r2, r3, s3, r4, fin, transit,
    ld_q, ld_g, ld_kv, st_att, st_dq, st_kv,
    z_s, t_s, t_r, own_s, rel_s, fwd_s, kr, fr, g1_s, g1_r, g2_s, g2_r, g3_r, g4_s, g4_r,
):
    c = lax.axis_index("ctx")
    z = lax.rem(c // 2, 2)
    core = lax.rem(c, 2)
    mate = c + 1 - 2 * core
    across = c + 2 - 4 * z

    def along_z(step):
        at = lax.rem(z * 8 + lax.axis_index("head") + step, 16)
        return {"ctx": c - 2 * z + 2 * (at // 8), "head": lax.rem(at, 8)}, at // 8

    ahead, z_ahead = along_z(4 + 8 * core)
    behind, _ = along_z(12 - 8 * core)
    low, high = pl.ds(0, T), pl.ds(T, T)

    def send(src, dst, ss, rs, dev):
        return pltpu.make_async_remote_copy(
            src_ref=src, dst_ref=dst, send_sem=ss, recv_sem=rs, device_id=dev if isinstance(dev, dict) else {"ctx": dev}, device_id_type=MESH
        )

    own_in = [
        pltpu.make_async_copy(src, kv.at[0, kind, low], ld_kv.at[kind]) for kind, src in enumerate((k_hbm, v_hbm))
    ]
    q_in = [
        pltpu.make_async_copy(q_hbm.at[:, pl.ds(h * D, D)], qs.at[pl.ds(h * T, T)], ld_q.at[h]) for h in range(G)
    ]
    g_in = [
        pltpu.make_async_copy(g_hbm.at[:, pl.ds(h * D, D)], gs.at[pl.ds(h * T, T)], ld_g.at[h]) for h in range(G)
    ]
    for copy in own_in:
        copy.start()

    barrier = pltpu.get_barrier_semaphore()
    for dev in ({"ctx": mate}, ahead, behind):
        pl.semaphore_signal(barrier, inc=1, device_id=dev, device_id_type=MESH)
    count = 3
    for d in range(1, 5):
        up, down = c + 4 * d < n_ctx, c - 4 * d >= 0
        count = count + up.astype(jnp.int32) + down.astype(jnp.int32)

        @pl.when(up)
        def _():
            pl.semaphore_signal(barrier, inc=1, device_id={"ctx": c + 4 * d}, device_id_type=MESH)

        @pl.when(down)
        def _():
            pl.semaphore_signal(barrier, inc=1, device_id={"ctx": c - 4 * d}, device_id_type=MESH)

    for copy in q_in + g_in:
        copy.start()

    for i in range(1, PAIRS):

        @pl.when(c < 2 * i)
        def _():
            kv[i] = jnp.zeros((2, 2 * T, D), BF16)

    for d in range(1, 5):

        @pl.when(c + 4 * d >= n_ctx)
        def _():
            r2[d] = jnp.zeros((2, D, T), BF16)

        @pl.when((c + 4 * d >= n_ctx) | (2 * d - 1 + 2 * z >= PAIRS))
        def _():
            r3[d] = jnp.zeros((2, D, T), BF16)

    for copy in own_in:
        copy.wait()
    pl.semaphore_wait(barrier, count)

    land = 9 - 8 * z_ahead
    here = 9 - 8 * z

    def z_send(kind):
        return send(kv.at[0, kind, low], transit.at[kind], z_s.at[kind], t_r.at[kind], ahead)

    def z_pass(kind):
        return send(transit.at[kind], kv.at[land, kind, low], t_s.at[kind], kr.at[land, kind], ahead)

    def pass_along(kind):
        z_send(kind).wait_recv()
        z_pass(kind).start()

    def own_send(d, kind):
        return send(
            kv.at[0, kind, low], kv.at[2 * d, kind, low], own_s.at[d, kind], kr.at[2 * d, kind], c + 4 * d
        )

    def relay_send(d, kind):
        to = 2 * d - 1 + 2 * z
        return send(kv.at[here, kind, low], kv.at[to, kind, low], rel_s.at[d, kind], kr.at[to, kind], c + 4 * d)

    def forward(i, kind):
        return send(kv.at[i, kind, low], kv.at[i, kind, high], fwd_s.at[i, kind], fr.at[i, kind], mate)

    def arrived(i, kind):
        return send(kv.at[i, kind, low], kv.at[i, kind, low], z_s.at[kind], kr.at[i, kind], mate)

    relays = lambda d: (c + 4 * d < n_ctx) & (2 * d - 1 + 2 * z < PAIRS)

    def start_sends(kind):
        z_send(kind).start()
        for d in (2, 1, 3, 4):

            @pl.when(c + 4 * d < n_ctx)
            def _():
                own_send(d, kind).start()

        forward(0, kind).start()

    start_sends(0)

    row = c * T + lax.broadcasted_iota(jnp.int32, (T, 2 * T), 0)
    lane = lax.broadcasted_iota(jnp.int32, (T, 2 * T), 1)
    doc = jnp.zeros((T, 2 * T), jnp.int32)
    start = jnp.int32(0)
    for j in range(lengths.shape[0]):
        doc = jnp.where(row >= start, start, doc)
        start = start + lengths[j]
    first = lane + jnp.where(lane < T, c * T, mate * T - T)

    def mask(i, _):
        key = first - i * (2 * T)
        bias[i] = jnp.where((key >= doc) & (key <= row), 0.0, NEG)
        return 0

    lax.fori_loop(0, PAIRS, mask, 0)
    for copy in q_in:
        copy.wait()
    m1[...] = jnp.full_like(m1, NEG)
    m2[...] = jnp.full_like(m2, NEG)
    for ref in (l1, l2, acc):
        ref[...] = jnp.zeros_like(ref)

    def scores(i, most):
        key = kv[i, 0]
        b = bias[i]
        b = jnp.concatenate([b, b], axis=0)
        for t in range(ROWS // CHUNK):
            rows = pl.ds(t * CHUNK, CHUNK)
            s = dot(qs[rows], key, NT) + b
            sbuf[i, rows] = s
            most[rows] = jnp.maximum(most[rows], jnp.maximum(s[:, :T], s[:, T:]))

    def wide(x):
        return jnp.concatenate([x, x], axis=1)

    def weigh(i, most, total):
        for t in range(ROWS // CHUNK):
            rows = pl.ds(t * CHUNK, CHUNK)
            p = jnp.exp2((sbuf[i, rows] - wide(most[rows])) * LOG2)
            total[rows] += p[:, :T] + p[:, T:]
            pbuf[i, rows] = p.astype(BF16)

    def spread(x):
        return jnp.broadcast_to(x, (x.shape[0], T))

    def take(i, kind):
        @pl.when(c >= 2 * i)
        def _():
            arrived(i, kind).wait_recv()
            forward(i, kind).start()

    def await_mate(i, kind):
        @pl.when(c >= 2 * i)
        def _():
            forward(i, kind).wait_recv()

    def near_scores(n, _):
        i = 2 * n

        @pl.when(n == 1)
        def _():
            start_sends(1)
            pass_along(0)

        @pl.when(n < 4)
        def _():
            take(i + 2, 0)

        await_mate(i, 0)
        scores(i, m1)
        return 0

    lax.fori_loop(0, 5, near_scores, 0)
    for h in range(G):
        rows = pl.ds(h * T, T)
        m1[rows] = spread(jnp.max(m1[rows], axis=1, keepdims=True))
        qt[:, rows] = qs[rows].T

    def near_weigh(n, _):
        i = 2 * n

        @pl.when(n < 4)
        def _():
            take(i + 2, 1)

        @pl.when(n == 2)
        def _():
            pass_along(1)

        await_mate(i, 1)
        weigh(i, m1, l1)
        for t in range(ROWS // CHUNK):
            rows = pl.ds(t * CHUNK, CHUNK)
            acc[rows] += dot(pbuf[i, rows], kv[i, 1], NN)
        return 0

    lax.fori_loop(0, 5, near_weigh, 0)
    for h in range(G):
        rows = pl.ds(h * T, T)
        l1[rows] = spread(jnp.sum(l1[rows], axis=1, keepdims=True))
    for copy in g_in:
        copy.wait()

    for kind in range(2):
        arrived(here, kind).wait_recv()
        for d in range(1, 5):

            @pl.when(relays(d))
            def _():
                relay_send(d, kind).start()

        @pl.when(z == 1)
        def _():
            forward(1, kind).start()

    @pl.when(z == 0)
    def _():
        take(1, 0)

    take(3, 0)

    def far_scores(n, _):
        i = 2 * n + 1

        @pl.when(n < 2)
        def _():
            take(i + 4, 0)

        await_mate(i, 0)
        scores(i, m2)
        return 0

    lax.fori_loop(0, 4, far_scores, 0)

    @pl.when(z == 0)
    def _():
        take(1, 1)

    for i in (3, 5, 7):
        take(i, 1)

    for h in range(G):
        rows = pl.ds(h * T, T)
        old = m1[rows]
        most = jnp.maximum(old, spread(jnp.max(m2[rows], axis=1, keepdims=True)))
        m2[rows] = most
        m1[rows] = jnp.exp2((old - most) * LOG2)

    def far_weigh(n, _):
        weigh(2 * n + 1, m2, l2)
        return 0

    lax.fori_loop(0, 4, far_weigh, 0)
    for h in range(G):
        rows = pl.ds(h * T, T)
        inverse = 1.0 / (m1[rows] * l1[rows] + spread(jnp.sum(l2[rows], axis=1, keepdims=True)))
        l2[rows] = inverse
        grad = (gs[rows].astype(F32) * inverse).astype(BF16)
        g2[rows] = grad
        gt[:, rows] = grad.T

    def swap(i, kind):
        return send(s1.at[i, kind], r1.at[i, kind], g1_s.at[i, kind], g1_r.at[i, kind], mate)

    def home(d, kind):
        return send(s2.at[2 * d, kind], r2.at[d, kind], g2_s.at[2 * d, kind], g2_r.at[d, kind], c - 4 * d)

    def to_relay(i, kind):
        d = (i + 1) // 2 - z
        return send(s2.at[i, kind], r3.at[d, kind], g2_s.at[i, kind], g3_r.at[d, kind], c - 4 * d)

    def back_across(kind):
        return send(s3.at[kind], r4.at[kind], g4_s.at[kind], g4_r.at[kind], across)

    def child(d):
        return (c + 4 * d < n_ctx) & (2 * d - 1 + 2 * z < PAIRS)

    def give(i, kind, value):
        part[i, kind] = value[:, :T]
        s1[i, kind] = value[:, T:].astype(BF16)

        @pl.when(c >= 2 * i)
        def _():
            swap(i, kind).start()

    def pass_far(i, kind):
        @pl.when(c >= 2 * i)
        def _():
            swap(i, kind).wait_recv()
            total = part[i, kind] + r1[i, kind].astype(F32)
            part[i, kind] = total
            s2[i, kind] = total.astype(BF16)

            @pl.when((z == 0) | (i > 1))
            def _():
                to_relay(i, kind).start()

    def pass_near(i):
        @pl.when(c >= 2 * i)
        def _():
            for kind in range(2):
                swap(i, kind).wait_recv()
                s2[i, kind] = (part[i, kind] + r1[i, kind].astype(F32)).astype(BF16)
                home(i // 2, kind).start()

    def relay_back(kind):
        for d in range(1, 5):

            @pl.when(child(d))
            def _():
                send(s2.at[0, kind], r3.at[d, kind], g2_s.at[0, kind], g3_r.at[d, kind], mate).wait_recv()

        total = r3[1, kind].astype(F32) + r3[2, kind].astype(F32) + r3[3, kind].astype(F32) + r3[4, kind].astype(F32)
        s3[kind] = (total + part[1, kind] * z.astype(F32)).astype(BF16)
        back_across(kind).start()

    def far_values(n, _):
        i = 2 * n + 1
        give(i, 1, dot(gt[...], pbuf[i], NN))
        return 0

    lax.fori_loop(0, 4, far_values, 0)

    for n in range(4):
        await_mate(2 * n + 1, 1)

    def attend(t, _):
        rows = pl.ds(pl.multiple_of(t * CHUNK, CHUNK), CHUNK)
        total = acc[rows] * m1[rows]
        for i in (1, 3, 5, 7):
            total = total + dot(pbuf[i, rows], kv[i, 1], NN)
        inverse = l2[rows]
        out = (total * inverse).astype(BF16)
        att[rows] = out
        delta = jnp.sum(g2[rows].astype(F32) * out.astype(F32), axis=1, keepdims=True)
        l1[rows] = spread(delta)
        return 0

    lax.fori_loop(0, ROWS // CHUNK, attend, 0)

    def pass_values(n, _):
        pass_far(2 * n + 1, 1)
        return 0

    lax.fori_loop(0, 4, pass_values, 0)

    def score_grads(i, grads, deltas):
        value = kv[i, 1]
        for t in range(ROWS // CHUNK):
            rows = pl.ds(t * CHUNK, CHUNK)
            ds = dot(grads[rows], value, NT) - wide(deltas[rows])
            dsb[i, rows] = (pbuf[i, rows].astype(F32) * ds).astype(BF16)
        give(i, 0, dot(qt[...], dsb[i], NN))

    def far_keys(n, _):
        score_grads(2 * n + 1, g2, l1)

        @pl.when(n > 1)
        def _():
            pass_far(2 * n - 3, 0)

        return 0

    lax.fori_loop(0, 4, far_keys, 0)
    att_out = [
        pltpu.make_async_copy(att.at[pl.ds(h * T, T)], att_hbm.at[:, pl.ds(h * D, D)], st_att.at[h]) for h in range(G)
    ]
    for copy in att_out:
        copy.start()
    for h in range(G):
        rows = pl.ds(h * T, T)
        grad = (gs[rows].astype(F32) * (l2[rows] * m1[rows])).astype(BF16)
        gs[rows] = grad
        gt[:, rows] = grad.T
        l1[rows] = spread(jnp.sum(grad.astype(F32) * att[rows].astype(F32), axis=1, keepdims=True))
    pass_far(5, 0)
    pass_far(7, 0)

    def near(n, _):
        i = 8 - 2 * n
        give(i, 1, dot(gt[...], pbuf[i], NN))
        score_grads(i, gs, l1)

        @pl.when(n == 1)
        def _():
            relay_back(1)

        @pl.when(n > 1)
        def _():
            pass_near(i + 4)

        @pl.when(n == 2)
        def _():
            relay_back(0)

        return 0

    lax.fori_loop(0, 5, near, 0)
    pass_near(2)

    def query_grads(t, _):
        rows = pl.ds(pl.multiple_of(t * CHUNK, CHUNK), CHUNK)
        total = dot(dsb[0, rows], kv[0, 0], NN)
        for i in range(1, PAIRS):
            total = total + dot(dsb[i, rows], kv[i, 0], NN)
        dqo[rows] = (total * SCALE).astype(BF16)
        return 0

    lax.fori_loop(0, ROWS // CHUNK, query_grads, 0)
    dq_out = [
        pltpu.make_async_copy(dqo.at[pl.ds(h * T, T)], dq_hbm.at[:, pl.ds(h * D, D)], st_dq.at[h]) for h in range(G)
    ]
    for copy in dq_out:
        copy.start()

    for kind in range(2):
        swap(0, kind).wait_recv()
        for d in range(1, 5):

            @pl.when(c + 4 * d < n_ctx)
            def _():
                send(s2.at[0, kind], r2.at[d, kind], g2_s.at[0, kind], g2_r.at[d, kind], mate).wait_recv()

        total = part[0, kind] + r1[0, kind].astype(F32)
        for d in range(1, 5):
            total = total + r2[d, kind].astype(F32)
        part[0, kind] = total
    for kind in range(2):
        z_send(kind).wait_send()
        z_pass(kind).wait_send()
        for d in range(1, 5):

            @pl.when(c + 4 * d < n_ctx)
            def _():
                own_send(d, kind).wait_send()

            @pl.when(relays(d))
            def _():
                relay_send(d, kind).wait_send()

        for i in range(PAIRS):

            @pl.when(c >= 2 * i)
            def _():
                forward(i, kind).wait_send()


    for i in range(PAIRS):

        @pl.when(c >= 2 * i)
        def _():
            for kind in range(2):
                swap(i, kind).wait_send()
                if i > 0 and i % 2 == 0:
                    home(i // 2, kind).wait_send()
                if i > 1 and i % 2 == 1:
                    to_relay(i, kind).wait_send()

    @pl.when((z == 0) & (c >= 2))
    def _():
        for kind in range(2):
            to_relay(1, kind).wait_send()

    for copy in att_out + dq_out:
        copy.wait()
    kv_out = [pltpu.make_async_copy(fin.at[j], ref, st_kv.at[j]) for j, ref in enumerate((dk_hbm, dv_hbm))]
    for kind in (1, 0):
        back_across(kind).wait_recv()
        total = part[0, kind] + r4[kind].astype(F32)
        fin[kind] = (total.T * (1.0 if kind else SCALE)).astype(BF16)
        kv_out[kind].start()

    for kind in range(2):
        back_across(kind).wait_send()
    for copy in kv_out:
        copy.wait()


def hand_over(*refs):
    sources, outs, held, sem_in, sem_out = refs[:4], refs[4:8], refs[8:12], refs[12], refs[13]
    into = [pltpu.make_async_copy(a, b, sem_in.at[j]) for j, (a, b) in enumerate(zip(sources, held))]
    out = [pltpu.make_async_copy(a, b, sem_out.at[j]) for j, (a, b) in enumerate(zip(held, outs))]
    for copy in into:
        copy.start()
    for first, second in zip(into, out):
        first.wait()
        second.start()
    for copy in out:
        copy.wait()


def solution(mesh):
    n_ctx = mesh.shape["ctx"]

    def on_device(queries, key_rows, value_rows, out_grad, doc_lengths):
        anywhere = pl.BlockSpec(memory_space=pl.ANY)
        dma = pltpu.SemaphoreType.DMA
        vmem = pltpu.VMEM
        shapes = (
                jax.ShapeDtypeStruct(queries.shape, BF16),
                jax.ShapeDtypeStruct(queries.shape, BF16),
                jax.ShapeDtypeStruct(key_rows.shape, BF16),
                jax.ShapeDtypeStruct(value_rows.shape, BF16),
        )
        results = pl.pallas_call(
            functools.partial(kernel, n_ctx),
            out_shape=shapes,
            in_specs=[anywhere] * 4 + [pl.BlockSpec(memory_space=pltpu.SMEM)],
            out_specs=(anywhere,) * 4,
            scratch_shapes=[
                vmem((PAIRS + 1, 2, 2 * T, D), BF16),
                vmem((ROWS, D), BF16),
                vmem((ROWS, D), BF16),
                vmem((ROWS, D), BF16),
                vmem((D, ROWS), BF16),
                vmem((D, ROWS), BF16),
                vmem((PAIRS, ROWS, 2 * T), F32),
                vmem((PAIRS, ROWS, 2 * T), BF16),
                vmem((PAIRS, ROWS, 2 * T), BF16),
                vmem((PAIRS, T, 2 * T), F32),
                vmem((ROWS, T), F32),
                vmem((ROWS, T), F32),
                vmem((ROWS, T), F32),
                vmem((ROWS, T), F32),
                vmem((ROWS, D), F32),
                vmem((ROWS, D), BF16),
                vmem((ROWS, D), BF16),
                vmem((PAIRS, 2, D, T), F32),
                vmem((PAIRS, 2, D, T), BF16),
                vmem((PAIRS, 2, D, T), BF16),
                vmem((PAIRS, 2, D, T), BF16),
                vmem((5, 2, D, T), BF16),
                vmem((5, 2, D, T), BF16),
                vmem((2, D, T), BF16),
                vmem((2, D, T), BF16),
                vmem((2, T, D), BF16),
                vmem((2, T, D), BF16),
                dma((G,)), dma((G,)), dma((2,)), dma((G,)), dma((G,)), dma((2,)),
                dma((2,)), dma((2,)), dma((2,)), dma((5, 2)), dma((5, 2)), dma((PAIRS, 2)), dma((PAIRS + 1, 2)), dma((PAIRS, 2)),
                dma((PAIRS, 2)), dma((PAIRS, 2)), dma((PAIRS, 2)), dma((5, 2)), dma((5, 2)), dma((2,)), dma((2,)),
            ],
            compiler_params=pltpu.CompilerParams(
                collective_id=0, has_side_effects=True, vmem_limit_bytes=60 * 1024 * 1024
            ),
        )(queries, key_rows, value_rows, out_grad, doc_lengths)
        return pl.pallas_call(
            hand_over,
            out_shape=shapes,
            in_specs=[anywhere] * 4,
            out_specs=(anywhere,) * 4,
            scratch_shapes=[vmem(x.shape, x.dtype) for x in shapes] + [dma((4,)), dma((4,))],
            compiler_params=pltpu.CompilerParams(vmem_limit_bytes=62 * 1024 * 1024),
        )(*results)

    split = P("ctx", "head")
    return jax.shard_map(
        on_device, mesh=mesh, in_specs=(split, split, split, split, P()), out_specs=(split,) * 4, check_vma=False
    )
```

```python
import functools
import math

import jax
import jax.numpy as jnp
from jax import lax
from jax.experimental import pallas as pl
from jax.experimental.pallas import tpu as pltpu
from jax.sharding import PartitionSpec as P

MESH = pl.DeviceIdType.MESH
T = 128
D = 128
G = 8
ROWS = T * G
PAIRS = 9
CHUNK = 256
NEG = -1e30
SCALE = D**-0.5
LOG2 = SCALE * math.log2(math.e)
NT = (((1,), (1,)), ((), ()))
NN = (((1,), (0,)), ((), ()))
F32, BF16 = jnp.float32, jnp.bfloat16


def dot(a, b, dims):
    return lax.dot_general(a, b, dims, preferred_element_type=F32)


def kernel(
    n_ctx,
    q_hbm, k_hbm, v_hbm, g_hbm, lengths,
    att_hbm, dq_hbm, sum_hbm, r4,
    kv, qs, gs, g2, qt, gt, sbuf, pbuf, dsb, bias, m1, m2, l1, l2, acc, att, dqo,
    part, s1, r1, s2, r2, r3, s3, transit,
    ld_q, ld_g, ld_kv, st_att, st_dq, st_kv,
    z_s, t_s, t_r, own_s, rel_s, fwd_s, kr, fr, g1_r, g2_r, g3_r, g4_r,
):
    c = lax.axis_index("ctx")
    z = lax.rem(c // 2, 2)
    core = lax.rem(c, 2)
    mate = c + 1 - 2 * core
    across = c + 2 - 4 * z

    def along_z(step):
        at = lax.rem(z * 8 + lax.axis_index("head") + step, 16)
        return {"ctx": c - 2 * z + 2 * (at // 8), "head": lax.rem(at, 8)}, at // 8

    ahead, z_ahead = along_z(4 + 8 * core)
    behind, _ = along_z(12 - 8 * core)
    low, high = pl.ds(0, T), pl.ds(T, T)

    def send(src, dst, ss, rs, dev):
        return pltpu.make_async_remote_copy(
            src_ref=src, dst_ref=dst, send_sem=ss, recv_sem=rs, device_id=dev if isinstance(dev, dict) else {"ctx": dev}, device_id_type=MESH
        )

    def whole(ref, sem):
        return pltpu.make_async_copy(ref, ref, sem)

    own_in = [
        pltpu.make_async_copy(src, kv.at[0, kind, low], ld_kv.at[kind]) for kind, src in enumerate((k_hbm, v_hbm))
    ]
    q_in = [
        pltpu.make_async_copy(q_hbm.at[:, pl.ds(h * D, D)], qs.at[pl.ds(h * T, T)], ld_q) for h in range(G)
    ]
    g_in = [
        pltpu.make_async_copy(g_hbm.at[:, pl.ds(h * D, D)], gs.at[pl.ds(h * T, T)], ld_g) for h in range(G)
    ]
    for copy in own_in:
        copy.start()

    barrier = pltpu.get_barrier_semaphore()
    for dev in ({"ctx": mate}, ahead, behind):
        pl.semaphore_signal(barrier, inc=1, device_id=dev, device_id_type=MESH)
    count = 3
    for d in range(1, 5):
        up, down = c + 4 * d < n_ctx, c - 4 * d >= 0
        count = count + up.astype(jnp.int32) + down.astype(jnp.int32)

        @pl.when(up)
        def _():
            pl.semaphore_signal(barrier, inc=1, device_id={"ctx": c + 4 * d}, device_id_type=MESH)

        @pl.when(down)
        def _():
            pl.semaphore_signal(barrier, inc=1, device_id={"ctx": c - 4 * d}, device_id_type=MESH)

    for copy in q_in + g_in:
        copy.start()

    for i in range(1, PAIRS):

        @pl.when(c < 2 * i)
        def _():
            kv[i] = jnp.zeros((2, 2 * T, D), BF16)

    for d in range(1, 5):

        @pl.when(c + 4 * d >= n_ctx)
        def _():
            r2[d] = jnp.zeros((2, D, T), BF16)

        @pl.when((c + 4 * d >= n_ctx) | (2 * d - 1 + 2 * z >= PAIRS))
        def _():
            r3[d] = jnp.zeros((2, D, T), BF16)

    for copy in own_in:
        copy.wait()
    pl.semaphore_wait(barrier, count)

    land = 9 - 8 * z_ahead
    here = 9 - 8 * z

    def z_send(kind):
        return send(kv.at[0, kind, low], transit.at[kind], z_s.at[kind], t_r.at[kind], ahead)

    def z_pass(kind):
        return send(transit.at[kind], kv.at[land, kind, low], t_s.at[kind], kr.at[far(land, kind)], ahead)

    def pass_along(kind):
        z_send(kind).wait_recv()
        z_pass(kind).start()

    def own_send(d, kind):
        at = 4 * kind + d - 1
        return send(kv.at[0, kind, low], kv.at[2 * d, kind, low], own_s.at[at], kr.at[at], c + 4 * d)

    def far(i, kind):
        return 8 + 5 * kind + (i - 1) // 2

    def far_swapped(i, kind):
        return 5 + 4 * kind + (i - 1) // 2

    def relay_send(d, kind):
        to = 2 * d - 1 + 2 * z
        return send(
            kv.at[here, kind, low], kv.at[to, kind, low], rel_s.at[4 * kind + d - 1], kr.at[far(to, kind)], c + 4 * d
        )

    def near_forward(i, kind):
        at = 5 * kind + i // 2
        return send(kv.at[i, kind, low], kv.at[i, kind, high], fwd_s.at[at], fr.at[at], mate)

    def far_forward(i, kind):
        at = far_swapped(i, kind) + 5
        return send(kv.at[i, kind, low], kv.at[i, kind, high], fwd_s.at[at], fr.at[at], mate)

    def near_arrived(i, kind):
        return send(kv.at[i, kind, low], kv.at[i, kind, low], z_s.at[0], kr.at[4 * kind + i // 2 - 1], mate)

    def far_arrived(i, kind):
        return send(kv.at[i, kind, low], kv.at[i, kind, low], z_s.at[kind], kr.at[far(i, kind)], mate)

    relays = lambda d: (c + 4 * d < n_ctx) & (2 * d - 1 + 2 * z < PAIRS)

    def start_sends(kind):
        z_send(kind).start()
        for d in (2, 1, 3, 4):

            @pl.when(c + 4 * d < n_ctx)
            def _():
                own_send(d, kind).start()

        near_forward(0, kind).start()

    start_sends(0)

    row = c * T + lax.broadcasted_iota(jnp.int32, (T, 2 * T), 0)
    lane = lax.broadcasted_iota(jnp.int32, (T, 2 * T), 1)
    doc = jnp.zeros((T, 2 * T), jnp.int32)
    start = jnp.int32(0)
    for j in range(lengths.shape[0]):
        doc = jnp.where(row >= start, start, doc)
        start = start + lengths[j]
    first = lane + jnp.where(lane < T, c * T, mate * T - T)

    def mask(i, _):
        key = first - i * (2 * T)
        bias[i] = jnp.where((key >= doc) & (key <= row), 0.0, NEG)
        return 0

    lax.fori_loop(0, PAIRS, mask, 0)
    whole(qs, ld_q).wait()
    m1[...] = jnp.full_like(m1, NEG)
    m2[...] = jnp.full_like(m2, NEG)
    for ref in (l1, l2, acc):
        ref[...] = jnp.zeros_like(ref)

    def scores(i, most):
        key = kv[i, 0]
        b = bias[i]
        b = jnp.concatenate([b, b], axis=0)
        for t in range(ROWS // CHUNK):
            rows = pl.ds(t * CHUNK, CHUNK)
            s = dot(qs[rows], key, NT) + b
            sbuf[i, rows] = s
            most[rows] = jnp.maximum(most[rows], jnp.maximum(s[:, :T], s[:, T:]))

    def wide(x):
        return jnp.concatenate([x, x], axis=1)

    def weigh(i, most, total):
        for t in range(ROWS // CHUNK):
            rows = pl.ds(t * CHUNK, CHUNK)
            p = jnp.exp2((sbuf[i, rows] - wide(most[rows])) * LOG2)
            total[rows] += p[:, :T] + p[:, T:]
            pbuf[i, rows] = p.astype(BF16)

    def spread(x):
        return jnp.broadcast_to(x, (x.shape[0], T))

    def take_near(i, kind):
        @pl.when(c >= 2 * i)
        def _():
            near_arrived(i, kind).wait_recv()
            near_forward(i, kind).start()

    def await_near(i, kind):
        @pl.when(c >= 2 * i)
        def _():
            near_forward(i, kind).wait_recv()

    def take_far(i, kind):
        @pl.when(c >= 2 * i)
        def _():
            far_arrived(i, kind).wait_recv()
            far_forward(i, kind).start()

    def await_far(i, kind):
        @pl.when(c >= 2 * i)
        def _():
            far_forward(i, kind).wait_recv()

    def near_scores(n, _):
        i = 2 * n

        @pl.when(n == 1)
        def _():
            start_sends(1)
            pass_along(0)

        @pl.when(n < 4)
        def _():
            take_near(i + 2, 0)

        await_near(i, 0)
        scores(i, m1)
        return 0

    lax.fori_loop(0, 5, near_scores, 0)
    for h in range(G):
        rows = pl.ds(h * T, T)
        m1[rows] = spread(jnp.max(m1[rows], axis=1, keepdims=True))
        qt[:, rows] = qs[rows].T

    def near_weigh(n, _):
        i = 2 * n

        @pl.when(n < 4)
        def _():
            take_near(i + 2, 1)

        @pl.when(n == 2)
        def _():
            pass_along(1)

        await_near(i, 1)
        weigh(i, m1, l1)
        for t in range(ROWS // CHUNK):
            rows = pl.ds(t * CHUNK, CHUNK)
            acc[rows] += dot(pbuf[i, rows], kv[i, 1], NN)
        return 0

    lax.fori_loop(0, 5, near_weigh, 0)
    for h in range(G):
        rows = pl.ds(h * T, T)
        l1[rows] = spread(jnp.sum(l1[rows], axis=1, keepdims=True))
    whole(gs, ld_g).wait()

    for kind in range(2):
        far_arrived(here, kind).wait_recv()
        for d in range(1, 5):

            @pl.when(relays(d))
            def _():
                relay_send(d, kind).start()

        @pl.when(z == 1)
        def _():
            far_forward(1, kind).start()

    @pl.when(z == 0)
    def _():
        take_far(1, 0)

    take_far(3, 0)

    def far_scores(n, _):
        i = 2 * n + 1

        @pl.when(n < 2)
        def _():
            take_far(i + 4, 0)

        await_far(i, 0)
        scores(i, m2)
        return 0

    lax.fori_loop(0, 4, far_scores, 0)

    @pl.when(z == 0)
    def _():
        take_far(1, 1)

    for i in (3, 5, 7):
        take_far(i, 1)

    for h in range(G):
        rows = pl.ds(h * T, T)
        old = m1[rows]
        most = jnp.maximum(old, spread(jnp.max(m2[rows], axis=1, keepdims=True)))
        m2[rows] = most
        m1[rows] = jnp.exp2((old - most) * LOG2)

    def far_weigh(n, _):
        weigh(2 * n + 1, m2, l2)
        return 0

    lax.fori_loop(0, 4, far_weigh, 0)
    for h in range(G):
        rows = pl.ds(h * T, T)
        inverse = 1.0 / (m1[rows] * l1[rows] + spread(jnp.sum(l2[rows], axis=1, keepdims=True)))
        l2[rows] = inverse
        grad = (gs[rows].astype(F32) * inverse).astype(BF16)
        g2[rows] = grad
        gt[:, rows] = grad.T

    def near_swap(i):
        return send(s1.at[i], r1.at[i], fwd_s.at[i // 2], g1_r.at[i // 2], mate)

    def far_swap(i, kind):
        return send(s1.at[i, kind], r1.at[i, kind], fwd_s.at[far_swapped(i, 1 - kind) + 5], g1_r.at[far_swapped(i, kind)], mate)

    def home(d):
        return send(s2.at[2 * d], r2.at[d], own_s.at[d - 1], g2_r.at[d - 1], c - 4 * d)

    def to_relay(i, kind):
        d = (i + 1) // 2 - z
        return send(
            s2.at[i, kind], r3.at[d, kind], rel_s.at[4 - 4 * kind + (i - 1) // 2], g3_r.at[4 * kind + d - 1], c - 4 * d
        )

    def back_across(kind):
        return send(s3.at[kind], r4.at[kind], z_s.at[kind], g4_r.at[kind], across)

    def gather_sent(kind):
        z_send(kind).wait_send()
        z_pass(kind).wait_send()
        for d in range(1, 5):

            @pl.when(relays(d))
            def _():
                relay_send(d, kind).wait_send()

        for i in (1, 3, 5, 7):

            @pl.when(c >= 2 * i)
            def _():
                far_forward(i, kind).wait_send()

    def near_sent():
        for d in range(1, 5):

            @pl.when(c + 4 * d < n_ctx)
            def _():
                for kind in range(2):
                    own_send(d, kind).wait_send()

        for i in range(0, PAIRS, 2):

            @pl.when(c >= 2 * i)
            def _():
                for kind in range(2):
                    near_forward(i, kind).wait_send()

    def child(d):
        return (c + 4 * d < n_ctx) & (2 * d - 1 + 2 * z < PAIRS)

    def keep(i, kind, value):
        part[i, kind] = value[:, :T]
        s1[i, kind] = value[:, T:].astype(BF16)

    def give(i, kind, value):
        keep(i, kind, value)

        @pl.when(c >= 2 * i)
        def _():
            far_swap(i, kind).start()

    def pass_far(i, kind):
        @pl.when(c >= 2 * i)
        def _():
            far_swap(i, kind).wait_recv()
            total = part[i, kind] + r1[i, kind].astype(F32)
            part[i, kind] = total
            s2[i, kind] = total.astype(BF16)

            @pl.when((z == 0) | (i > 1))
            def _():
                to_relay(i, kind).start()

    def pass_near(i):
        @pl.when(c >= 2 * i)
        def _():
            near_swap(i).wait_recv()
            s2[i] = (part[i] + r1[i].astype(F32)).astype(BF16)
            home(i // 2).start()

    def relay_back(kind):
        for d in range(1, 5):

            @pl.when(child(d))
            def _():
                send(s2.at[0, kind], r3.at[d, kind], z_s.at[kind], g3_r.at[4 * kind + d - 1], mate).wait_recv()

        total = r3[1, kind].astype(F32) + r3[2, kind].astype(F32) + r3[3, kind].astype(F32) + r3[4, kind].astype(F32)
        s3[kind] = (total + part[1, kind] * z.astype(F32)).astype(BF16)
        back_across(kind).start()

    def far_pair(n):
        up = jnp.where(n == 0, 3, jnp.where(n == 1, 5, jnp.where(n == 2, 1, 7)))
        down = jnp.where(n == 0, 5, jnp.where(n == 1, 7, jnp.where(n == 2, 3, 1)))
        return jnp.where(z == 0, up, down)

    def far_values(n, _):
        i = far_pair(n)
        give(i, 1, dot(gt[...], pbuf[i], NN))
        return 0

    gather_sent(0)
    lax.fori_loop(0, 4, far_values, 0)

    for n in range(4):
        await_far(2 * n + 1, 1)

    def attend(t, _):
        rows = pl.ds(pl.multiple_of(t * CHUNK, CHUNK), CHUNK)
        total = acc[rows] * m1[rows]
        for i in (1, 3, 5, 7):
            total = total + dot(pbuf[i, rows], kv[i, 1], NN)
        inverse = l2[rows]
        out = (total * inverse).astype(BF16)
        att[rows] = out
        delta = jnp.sum(g2[rows].astype(F32) * out.astype(F32), axis=1, keepdims=True)
        l1[rows] = spread(delta)
        return 0

    lax.fori_loop(0, ROWS // CHUNK, attend, 0)

    def pass_values(n, _):
        pass_far(far_pair(n), 1)
        return 0

    lax.fori_loop(0, 4, pass_values, 0)

    def score_grads(i, grads, deltas, after):
        value = kv[i, 1]
        for t in range(ROWS // CHUNK):
            rows = pl.ds(t * CHUNK, CHUNK)
            ds = dot(grads[rows], value, NT) - wide(deltas[rows])
            dsb[i, rows] = (pbuf[i, rows].astype(F32) * ds).astype(BF16)
        after(i, 0, dot(qt[...], dsb[i], NN))

    def far_keys(n, _):
        score_grads(far_pair(n), g2, l1, give)

        @pl.when(n > 1)
        def _():
            pass_far(far_pair(n - 2), 0)

        return 0

    gather_sent(1)
    lax.fori_loop(0, 4, far_keys, 0)
    near_sent()
    att_out = [
        pltpu.make_async_copy(att.at[pl.ds(h * T, T)], att_hbm.at[:, pl.ds(h * D, D)], st_att) for h in range(G)
    ]
    for copy in att_out:
        copy.start()
    for h in range(G):
        rows = pl.ds(h * T, T)
        grad = (gs[rows].astype(F32) * (l2[rows] * m1[rows])).astype(BF16)
        gs[rows] = grad
        gt[:, rows] = grad.T
        l1[rows] = spread(jnp.sum(grad.astype(F32) * att[rows].astype(F32), axis=1, keepdims=True))
    pass_far(far_pair(2), 0)
    pass_far(far_pair(3), 0)

    def near(n, _):
        i = 8 - 2 * n
        keep(i, 1, dot(gt[...], pbuf[i], NN))
        score_grads(i, gs, l1, keep)

        @pl.when(c >= 2 * i)
        def _():
            near_swap(i).start()

        @pl.when(n == 1)
        def _():
            relay_back(1)

        @pl.when(n > 1)
        def _():
            pass_near(i + 4)

        @pl.when(n == 2)
        def _():
            relay_back(0)

        return 0

    lax.fori_loop(0, 5, near, 0)
    pass_near(2)

    def query_grads(t, _):
        rows = pl.ds(pl.multiple_of(t * CHUNK, CHUNK), CHUNK)
        total = dot(dsb[0, rows], kv[0, 0], NN)
        for i in range(1, PAIRS):
            total = total + dot(dsb[i, rows], kv[i, 0], NN)
        dqo[rows] = (total * SCALE).astype(BF16)
        return 0

    lax.fori_loop(0, ROWS // CHUNK, query_grads, 0)
    dq_out = [
        pltpu.make_async_copy(dqo.at[pl.ds(h * T, T)], dq_hbm.at[:, pl.ds(h * D, D)], st_dq) for h in range(G)
    ]
    for copy in dq_out:
        copy.start()

    near_swap(0).wait_recv()
    for d in range(1, 5):

        @pl.when(c + 4 * d < n_ctx)
        def _():
            send(s2.at[0], r2.at[d], z_s.at[0], g2_r.at[d - 1], mate).wait_recv()

    for kind in range(2):
        total = part[0, kind] + r1[0, kind].astype(F32)
        for d in range(1, 5):
            total = total + r2[d, kind].astype(F32)
        part[0, kind] = total

    for i in range(PAIRS):

        @pl.when(c >= 2 * i)
        def _():
            if i % 2 == 0:
                near_swap(i).wait_send()
                if i > 0:
                    home(i // 2).wait_send()
            else:
                for kind in range(2):
                    far_swap(i, kind).wait_send()
                    if i > 1:
                        to_relay(i, kind).wait_send()

    @pl.when((z == 0) & (c >= 2))
    def _():
        for kind in range(2):
            to_relay(1, kind).wait_send()

    sums_out = pltpu.make_async_copy(part.at[0], sum_hbm, st_kv)
    sums_out.start()
    for copy in (whole(att, st_att), whole(dqo, st_dq), sums_out):
        copy.wait()
    for kind in range(2):
        back_across(kind).wait_send()
    for kind in (1, 0):
        back_across(kind).wait_recv()


def finish(att_in, dq_in, sums_in, back_in, att_out, dq_out, dk_out, dv_out, att, dq, sums, back, out, sem_in, sem_out):
    def copies(pairs, sems):
        return [pltpu.make_async_copy(a, b, sems.at[j]) for j, (a, b) in enumerate(pairs)]

    into = copies(((back_in, back), (sums_in, sums), (att_in, att), (dq_in, dq)), sem_in)
    away = copies(((out.at[0], dk_out), (out.at[1], dv_out), (att, att_out), (dq, dq_out)), sem_out)
    for copy in into:
        copy.start()
    into[0].wait()
    into[1].wait()
    for kind, scale in enumerate((SCALE, 1.0)):
        total = sums[kind] + back[kind].astype(F32)
        out[kind] = (total.T * scale).astype(BF16)
        away[kind].start()
    for j in (2, 3):
        into[j].wait()
        away[j].start()
    for copy in away:
        copy.wait()


def solution(mesh):
    n_ctx = mesh.shape["ctx"]

    def on_device(queries, key_rows, value_rows, out_grad, doc_lengths):
        anywhere = pl.BlockSpec(memory_space=pl.ANY)
        dma = pltpu.SemaphoreType.DMA
        vmem = pltpu.VMEM
        wide = jax.ShapeDtypeStruct(queries.shape, BF16)
        narrow = jax.ShapeDtypeStruct(key_rows.shape, BF16)
        results = pl.pallas_call(
            functools.partial(kernel, n_ctx),
            out_shape=(wide, wide, jax.ShapeDtypeStruct((2, D, T), F32), jax.ShapeDtypeStruct((2, D, T), BF16)),
            in_specs=[anywhere] * 4 + [pl.BlockSpec(memory_space=pltpu.SMEM)],
            out_specs=(anywhere,) * 4,
            scratch_shapes=[
                vmem((PAIRS + 1, 2, 2 * T, D), BF16),
                vmem((ROWS, D), BF16),
                vmem((ROWS, D), BF16),
                vmem((ROWS, D), BF16),
                vmem((D, ROWS), BF16),
                vmem((D, ROWS), BF16),
                vmem((PAIRS, ROWS, 2 * T), F32),
                vmem((PAIRS, ROWS, 2 * T), BF16),
                vmem((PAIRS, ROWS, 2 * T), BF16),
                vmem((PAIRS, T, 2 * T), F32),
                vmem((ROWS, T), F32),
                vmem((ROWS, T), F32),
                vmem((ROWS, T), F32),
                vmem((ROWS, T), F32),
                vmem((ROWS, D), F32),
                vmem((ROWS, D), BF16),
                vmem((ROWS, D), BF16),
                vmem((PAIRS, 2, D, T), F32),
                vmem((PAIRS, 2, D, T), BF16),
                vmem((PAIRS, 2, D, T), BF16),
                vmem((PAIRS, 2, D, T), BF16),
                vmem((5, 2, D, T), BF16),
                vmem((5, 2, D, T), BF16),
                vmem((2, D, T), BF16),
                vmem((2, T, D), BF16),
                dma, dma, dma((2,)), dma, dma, dma,
                dma((2,)), dma((2,)), dma((2,)), dma((8,)), dma((8,)), dma((18,)), dma((18,)), dma((18,)),
                dma((13,)), dma((4,)), dma((8,)), dma((2,)),
            ],
            compiler_params=pltpu.CompilerParams(
                collective_id=0, has_side_effects=True, vmem_limit_bytes=60 * 1024 * 1024
            ),
        )(queries, key_rows, value_rows, out_grad, doc_lengths)
        return pl.pallas_call(
            finish,
            out_shape=(wide, wide, narrow, narrow),
            in_specs=[anywhere] * 4,
            out_specs=(anywhere,) * 4,
            scratch_shapes=[
                vmem(wide.shape, BF16), vmem(wide.shape, BF16), vmem((2, D, T), F32), vmem((2, D, T), BF16),
                vmem((2, T, D), BF16), dma((4,)), dma((4,)),
            ],
            compiler_params=pltpu.CompilerParams(vmem_limit_bytes=62 * 1024 * 1024),
        )(*results)

    split = P("ctx", "head")
    return jax.shard_map(
        on_device, mesh=mesh, in_specs=(split, split, split, split, P()), out_specs=(split,) * 4, check_vma=False
    )
```

```python
import functools
import math

import jax
import jax.numpy as jnp
from jax import lax
from jax.experimental import pallas as pl
from jax.experimental.pallas import tpu as pltpu
from jax.sharding import PartitionSpec as P

MESH = pl.DeviceIdType.MESH
T = 128
D = 128
G = 8
ROWS = T * G
PAIRS = 9
CHUNK = 256
NEG = -1e30
SCALE = D**-0.5
LOG2 = SCALE * math.log2(math.e)
NT = (((1,), (1,)), ((), ()))
NN = (((1,), (0,)), ((), ()))
F32, BF16 = jnp.float32, jnp.bfloat16


def dot(a, b, dims):
    return lax.dot_general(a, b, dims, preferred_element_type=F32)


def kernel(
    n_ctx,
    q_hbm, k_hbm, v_hbm, g_hbm, lengths,
    att_hbm, dq_hbm, sum_hbm, r4,
    kv, qs, gs, g2, qt, gt, sbuf, pbuf, dsb, bias, m1, m2, l1, l2, acc, att, dqo,
    part, s1, r1, s2, r2, r3, s3, transit,
    ld_q, ld_g, ld_kv, st_att, st_dq, st_kv,
    z_s, t_s, t_r, own_s, rel_s, fwd_s, kr, fr, g1_r, g2_r, g3_r, g4_r,
):
    c = lax.axis_index("ctx")
    z = lax.rem(c // 2, 2)
    core = lax.rem(c, 2)
    mate = c + 1 - 2 * core
    across = c + 2 - 4 * z

    def along_z(step):
        at = lax.rem(z * 8 + lax.axis_index("head") + step, 16)
        return {"ctx": c - 2 * z + 2 * (at // 8), "head": lax.rem(at, 8)}, at // 8

    ahead, z_ahead = along_z(4 + 8 * core)
    behind, _ = along_z(12 - 8 * core)
    low, high = pl.ds(0, T), pl.ds(T, T)

    def send(src, dst, ss, rs, dev):
        return pltpu.make_async_remote_copy(
            src_ref=src, dst_ref=dst, send_sem=ss, recv_sem=rs, device_id=dev if isinstance(dev, dict) else {"ctx": dev}, device_id_type=MESH
        )

    def whole(ref, sem):
        return pltpu.make_async_copy(ref, ref, sem)

    own_in = [
        pltpu.make_async_copy(src, kv.at[0, kind, low], ld_kv.at[kind]) for kind, src in enumerate((k_hbm, v_hbm))
    ]
    q_in = [
        pltpu.make_async_copy(q_hbm.at[:, pl.ds(h * D, D)], qs.at[pl.ds(h * T, T)], ld_q) for h in range(G)
    ]
    g_in = [
        pltpu.make_async_copy(g_hbm.at[:, pl.ds(h * D, D)], gs.at[pl.ds(h * T, T)], ld_g) for h in range(G)
    ]
    for copy in own_in:
        copy.start()

    barrier = pltpu.get_barrier_semaphore()
    for dev in ({"ctx": mate}, behind):
        pl.semaphore_signal(barrier, inc=1, device_id=dev, device_id_type=MESH)
    count = 2
    for d in range(1, 5):
        count = count + (c + 4 * d < n_ctx).astype(jnp.int32)

        @pl.when(c - 4 * d >= 0)
        def _():
            pl.semaphore_signal(barrier, inc=1, device_id={"ctx": c - 4 * d}, device_id_type=MESH)

    for copy in own_in:
        copy.wait()
    pl.semaphore_wait(barrier, count)

    land = 9 - 8 * z_ahead
    here = 9 - 8 * z

    def z_send(kind):
        return send(kv.at[0, kind, low], transit.at[kind], z_s.at[kind], t_r.at[kind], ahead)

    def z_pass(kind):
        return send(transit.at[kind], kv.at[land, kind, low], t_s.at[kind], kr.at[far(land, kind)], ahead)

    def pass_along(kind):
        z_send(kind).wait_recv()
        z_pass(kind).start()

    def own_send(d, kind):
        at = 4 * kind + d - 1
        return send(kv.at[0, kind, low], kv.at[2 * d, kind, low], own_s.at[at], kr.at[at], c + 4 * d)

    def far(i, kind):
        return 8 + 5 * kind + (i - 1) // 2

    def far_swapped(i, kind):
        return 5 + 4 * kind + (i - 1) // 2

    def relay_send(d, kind):
        to = 2 * d - 1 + 2 * z
        return send(
            kv.at[here, kind, low], kv.at[to, kind, low], rel_s.at[4 * kind + d - 1], kr.at[far(to, kind)], c + 4 * d
        )

    def near_forward(i, kind):
        at = 5 * kind + i // 2
        return send(kv.at[i, kind, low], kv.at[i, kind, high], fwd_s.at[at], fr.at[at], mate)

    def far_forward(i, kind):
        at = far_swapped(i, kind) + 5
        return send(kv.at[i, kind, low], kv.at[i, kind, high], fwd_s.at[at], fr.at[at], mate)

    def near_arrived(i, kind):
        return send(kv.at[i, kind, low], kv.at[i, kind, low], z_s.at[0], kr.at[4 * kind + i // 2 - 1], mate)

    def far_arrived(i, kind):
        return send(kv.at[i, kind, low], kv.at[i, kind, low], z_s.at[kind], kr.at[far(i, kind)], mate)

    relays = lambda d: (c + 4 * d < n_ctx) & (2 * d - 1 + 2 * z < PAIRS)

    def start_sends(kind):
        z_send(kind).start()
        for d in (2, 1, 3, 4):

            @pl.when(c + 4 * d < n_ctx)
            def _():
                own_send(d, kind).start()

        near_forward(0, kind).start()

    start_sends(0)
    for copy in q_in + g_in:
        copy.start()

    for i in range(1, PAIRS):

        @pl.when(c < 2 * i)
        def _():
            kv[i] = jnp.zeros((2, 2 * T, D), BF16)

    for d in range(1, 5):

        @pl.when(c + 4 * d >= n_ctx)
        def _():
            r2[d] = jnp.zeros((2, D, T), BF16)

        @pl.when((c + 4 * d >= n_ctx) | (2 * d - 1 + 2 * z >= PAIRS))
        def _():
            r3[d] = jnp.zeros((2, D, T), BF16)

    row = c * T + lax.broadcasted_iota(jnp.int32, (T, 2 * T), 0)
    lane = lax.broadcasted_iota(jnp.int32, (T, 2 * T), 1)
    doc = jnp.zeros((T, 2 * T), jnp.int32)
    start = jnp.int32(0)
    for j in range(lengths.shape[0]):
        doc = jnp.where(row >= start, start, doc)
        start = start + lengths[j]
    first = lane + jnp.where(lane < T, c * T, mate * T - T)

    def mask(i, _):
        key = first - i * (2 * T)
        bias[i] = jnp.where((key >= doc) & (key <= row), 0.0, NEG)
        return 0

    lax.fori_loop(0, PAIRS, mask, 0)
    whole(qs, ld_q).wait()
    m1[...] = jnp.full_like(m1, NEG)
    m2[...] = jnp.full_like(m2, NEG)
    for ref in (l1, l2, acc):
        ref[...] = jnp.zeros_like(ref)

    def scores(i, most):
        key = kv[i, 0]
        b = bias[i]
        b = jnp.concatenate([b, b], axis=0)
        for t in range(ROWS // CHUNK):
            rows = pl.ds(t * CHUNK, CHUNK)
            s = dot(qs[rows], key, NT) + b
            sbuf[i, rows] = s
            most[rows] = jnp.maximum(most[rows], jnp.maximum(s[:, :T], s[:, T:]))

    def wide(x):
        return jnp.concatenate([x, x], axis=1)

    def weigh(i, most, total):
        for t in range(ROWS // CHUNK):
            rows = pl.ds(t * CHUNK, CHUNK)
            p = jnp.exp2((sbuf[i, rows] - wide(most[rows])) * LOG2)
            total[rows] += p[:, :T] + p[:, T:]
            pbuf[i, rows] = p.astype(BF16)

    def spread(x):
        return jnp.broadcast_to(x, (x.shape[0], T))

    def take_near(i, kind):
        @pl.when(c >= 2 * i)
        def _():
            near_arrived(i, kind).wait_recv()
            near_forward(i, kind).start()

    def await_near(i, kind):
        @pl.when(c >= 2 * i)
        def _():
            near_forward(i, kind).wait_recv()

    def take_far(i, kind):
        @pl.when(c >= 2 * i)
        def _():
            far_arrived(i, kind).wait_recv()
            far_forward(i, kind).start()

    def await_far(i, kind):
        @pl.when(c >= 2 * i)
        def _():
            far_forward(i, kind).wait_recv()

    def near_pair(n):
        return jnp.where(n < 2, 2 * n, 12 - 2 * n)

    def near_scores(n, _):
        i = near_pair(n)

        @pl.when(n == 1)
        def _():
            start_sends(1)
            pass_along(0)

        @pl.when(n < 4)
        def _():
            take_near(near_pair(n + 1), 0)

        await_near(i, 0)
        scores(i, m1)
        return 0

    lax.fori_loop(0, 5, near_scores, 0)
    for h in range(G):
        rows = pl.ds(h * T, T)
        m1[rows] = spread(jnp.max(m1[rows], axis=1, keepdims=True))
        qt[:, rows] = qs[rows].T

    def near_weigh(n, _):
        i = near_pair(n)

        @pl.when(n < 4)
        def _():
            take_near(near_pair(n + 1), 1)

        @pl.when(n == 1)
        def _():
            pass_along(1)

        await_near(i, 1)
        weigh(i, m1, l1)
        for t in range(ROWS // CHUNK):
            rows = pl.ds(t * CHUNK, CHUNK)
            acc[rows] += dot(pbuf[i, rows], kv[i, 1], NN)
        return 0

    lax.fori_loop(0, 5, near_weigh, 0)
    for h in range(G):
        rows = pl.ds(h * T, T)
        l1[rows] = spread(jnp.sum(l1[rows], axis=1, keepdims=True))
    whole(gs, ld_g).wait()

    def cross(kind):
        far_arrived(here, kind).wait_recv()
        for d in (2, 1, 3, 4):

            @pl.when(relays(d))
            def _():
                relay_send(d, kind).start()

        @pl.when(z == 1)
        def _():
            far_forward(1, kind).start()

    cross(0)

    @pl.when(z == 0)
    def _():
        take_far(1, 0)

    def far_arrival(n):
        up = jnp.where(n == 0, 1, 9 - 2 * n)
        down = jnp.where(n == 0, 1, jnp.where(n == 1, 3, 11 - 2 * n))
        return jnp.where(z == 0, up, down)

    take_far(far_arrival(1), 0)

    def far_scores(n, _):
        i = far_arrival(n)

        @pl.when(n < 2)
        def _():
            take_far(far_arrival(n + 2), 0)

        @pl.when(n == 1)
        def _():
            cross(1)

        await_far(i, 0)
        scores(i, m2)
        return 0

    lax.fori_loop(0, 4, far_scores, 0)

    @pl.when(z == 0)
    def _():
        take_far(1, 1)

    for n in (1, 2, 3):
        take_far(far_arrival(n), 1)

    for h in range(G):
        rows = pl.ds(h * T, T)
        old = m1[rows]
        most = jnp.maximum(old, spread(jnp.max(m2[rows], axis=1, keepdims=True)))
        m2[rows] = most
        m1[rows] = jnp.exp2((old - most) * LOG2)

    def far_weigh(n, _):
        weigh(2 * n + 1, m2, l2)
        return 0

    lax.fori_loop(0, 4, far_weigh, 0)
    for h in range(G):
        rows = pl.ds(h * T, T)
        inverse = 1.0 / (m1[rows] * l1[rows] + spread(jnp.sum(l2[rows], axis=1, keepdims=True)))
        l2[rows] = inverse
        grad = (gs[rows].astype(F32) * inverse).astype(BF16)
        g2[rows] = grad
        gt[:, rows] = grad.T

    def near_swap(i):
        return send(s1.at[i], r1.at[i], fwd_s.at[i // 2], g1_r.at[i // 2], mate)

    def far_swap(i, kind):
        return send(s1.at[i, kind], r1.at[i, kind], fwd_s.at[far_swapped(i, 1 - kind) + 5], g1_r.at[far_swapped(i, kind)], mate)

    def home(d):
        return send(s2.at[2 * d], r2.at[d], own_s.at[d - 1], g2_r.at[d - 1], c - 4 * d)

    def to_relay(i, kind):
        d = (i + 1) // 2 - z
        return send(
            s2.at[i, kind], r3.at[d, kind], rel_s.at[4 - 4 * kind + (i - 1) // 2], g3_r.at[4 * kind + d - 1], c - 4 * d
        )

    def back_across(kind):
        return send(s3.at[kind], r4.at[kind], z_s.at[kind], g4_r.at[kind], across)

    def gather_sent(kind):
        z_send(kind).wait_send()
        z_pass(kind).wait_send()
        for d in range(1, 5):

            @pl.when(relays(d))
            def _():
                relay_send(d, kind).wait_send()

        for i in (1, 3, 5, 7):

            @pl.when(c >= 2 * i)
            def _():
                far_forward(i, kind).wait_send()

    def near_sent():
        for d in range(1, 5):

            @pl.when(c + 4 * d < n_ctx)
            def _():
                for kind in range(2):
                    own_send(d, kind).wait_send()

        for i in range(0, PAIRS, 2):

            @pl.when(c >= 2 * i)
            def _():
                for kind in range(2):
                    near_forward(i, kind).wait_send()

    def child(d):
        return (c + 4 * d < n_ctx) & (2 * d - 1 + 2 * z < PAIRS)

    def keep(i, kind, value):
        part[i, kind] = value[:, :T]
        s1[i, kind] = value[:, T:].astype(BF16)

    def give(i, kind, value):
        keep(i, kind, value)

        @pl.when(c >= 2 * i)
        def _():
            far_swap(i, kind).start()

    def pass_far(i, kind):
        @pl.when(c >= 2 * i)
        def _():
            far_swap(i, kind).wait_recv()
            total = part[i, kind] + r1[i, kind].astype(F32)
            part[i, kind] = total
            s2[i, kind] = total.astype(BF16)

            @pl.when((z == 0) | (i > 1))
            def _():
                to_relay(i, kind).start()

    def pass_near(i):
        @pl.when(c >= 2 * i)
        def _():
            near_swap(i).wait_recv()
            s2[i] = (part[i] + r1[i].astype(F32)).astype(BF16)
            home(i // 2).start()

    def relay_back(kind):
        for d in range(1, 5):

            @pl.when(child(d))
            def _():
                send(s2.at[0, kind], r3.at[d, kind], z_s.at[kind], g3_r.at[4 * kind + d - 1], mate).wait_recv()

        total = r3[1, kind].astype(F32) + r3[2, kind].astype(F32) + r3[3, kind].astype(F32) + r3[4, kind].astype(F32)
        s3[kind] = (total + part[1, kind] * z.astype(F32)).astype(BF16)
        back_across(kind).start()

    def far_pair(n):
        up = jnp.where(n == 0, 3, jnp.where(n == 1, 5, jnp.where(n == 2, 1, 7)))
        down = jnp.where(n == 0, 5, jnp.where(n == 1, 7, jnp.where(n == 2, 3, 1)))
        return jnp.where(z == 0, up, down)

    def far_values(n, _):
        i = far_pair(n)
        give(i, 1, dot(gt[...], pbuf[i], NN))
        return 0

    gather_sent(0)
    lax.fori_loop(0, 4, far_values, 0)

    for n in range(4):
        await_far(2 * n + 1, 1)

    def attend(t, _):
        rows = pl.ds(pl.multiple_of(t * CHUNK, CHUNK), CHUNK)
        weights = jnp.concatenate([pbuf[i, rows] for i in (1, 3, 5, 7)], axis=1)
        values = jnp.concatenate([kv[i, 1] for i in (1, 3, 5, 7)], axis=0)
        total = acc[rows] * m1[rows] + dot(weights, values, NN)
        inverse = l2[rows]
        out = (total * inverse).astype(BF16)
        att[rows] = out
        delta = jnp.sum(g2[rows].astype(F32) * out.astype(F32), axis=1, keepdims=True)
        l1[rows] = spread(delta)
        return 0

    lax.fori_loop(0, ROWS // CHUNK, attend, 0)

    def pass_values(n, _):
        pass_far(far_pair(n), 1)
        return 0

    lax.fori_loop(0, 4, pass_values, 0)

    def score_grads(i, grads, deltas, after):
        value = kv[i, 1]
        for t in range(ROWS // CHUNK):
            rows = pl.ds(t * CHUNK, CHUNK)
            ds = dot(grads[rows], value, NT) - wide(deltas[rows])
            dsb[i, rows] = (pbuf[i, rows].astype(F32) * ds).astype(BF16)
        after(i, 0, dot(qt[...], dsb[i], NN))

    def far_keys(n, _):
        score_grads(far_pair(n), g2, l1, give)

        @pl.when(n > 1)
        def _():
            pass_far(far_pair(n - 2), 0)

        return 0

    gather_sent(1)
    lax.fori_loop(0, 4, far_keys, 0)
    near_sent()
    att_out = [
        pltpu.make_async_copy(att.at[pl.ds(h * T, T)], att_hbm.at[:, pl.ds(h * D, D)], st_att) for h in range(G)
    ]
    for copy in att_out:
        copy.start()
    for h in range(G):
        rows = pl.ds(h * T, T)
        grad = (gs[rows].astype(F32) * (l2[rows] * m1[rows])).astype(BF16)
        gs[rows] = grad
        gt[:, rows] = grad.T
        l1[rows] = spread(jnp.sum(grad.astype(F32) * att[rows].astype(F32), axis=1, keepdims=True))
    pass_far(far_pair(2), 0)
    pass_far(far_pair(3), 0)

    def near(n, _):
        i = 8 - 2 * n
        keep(i, 1, dot(gt[...], pbuf[i], NN))
        score_grads(i, gs, l1, keep)

        @pl.when(c >= 2 * i)
        def _():
            near_swap(i).start()

        @pl.when(n == 0)
        def _():
            relay_back(1)

        @pl.when(n > 1)
        def _():
            pass_near(i + 4)

        @pl.when(n == 2)
        def _():
            relay_back(0)

        return 0

    lax.fori_loop(0, 5, near, 0)
    pass_near(2)

    def query_grads(t, _):
        rows = pl.ds(pl.multiple_of(t * CHUNK, CHUNK), CHUNK)
        grads = jnp.concatenate([dsb[i, rows] for i in range(PAIRS)], axis=1)
        keys = jnp.concatenate([kv[i, 0] for i in range(PAIRS)], axis=0)
        total = dot(grads, keys, NN)
        dqo[rows] = (total * SCALE).astype(BF16)
        return 0

    lax.fori_loop(0, ROWS // CHUNK, query_grads, 0)
    dq_out = [
        pltpu.make_async_copy(dqo.at[pl.ds(h * T, T)], dq_hbm.at[:, pl.ds(h * D, D)], st_dq) for h in range(G)
    ]
    for copy in dq_out:
        copy.start()

    near_swap(0).wait_recv()
    for d in range(1, 5):

        @pl.when(c + 4 * d < n_ctx)
        def _():
            send(s2.at[0], r2.at[d], z_s.at[0], g2_r.at[d - 1], mate).wait_recv()

    for kind in range(2):
        total = part[0, kind] + r1[0, kind].astype(F32)
        for d in range(1, 5):
            total = total + r2[d, kind].astype(F32)
        part[0, kind] = total

    for i in range(PAIRS):

        @pl.when(c >= 2 * i)
        def _():
            if i % 2 == 0:
                near_swap(i).wait_send()
                if i > 0:
                    home(i // 2).wait_send()
            else:
                for kind in range(2):
                    far_swap(i, kind).wait_send()
                    if i > 1:
                        to_relay(i, kind).wait_send()

    @pl.when((z == 0) & (c >= 2))
    def _():
        for kind in range(2):
            to_relay(1, kind).wait_send()

    sums_out = pltpu.make_async_copy(part.at[0], sum_hbm, st_kv)
    sums_out.start()
    for copy in (whole(att, st_att), whole(dqo, st_dq), sums_out):
        copy.wait()
    for kind in range(2):
        back_across(kind).wait_send()
    for kind in (1, 0):
        back_across(kind).wait_recv()


def finish(att_in, dq_in, sums_in, back_in, att_out, dq_out, dk_out, dv_out, att, dq, sums, back, out, sem_in, sem_out):
    def copies(pairs, sems):
        return [pltpu.make_async_copy(a, b, sems.at[j]) for j, (a, b) in enumerate(pairs)]

    into = copies(((back_in, back), (sums_in, sums), (att_in, att), (dq_in, dq)), sem_in)
    away = copies(((out.at[0], dk_out), (out.at[1], dv_out), (att, att_out), (dq, dq_out)), sem_out)
    for copy in into:
        copy.start()
    into[0].wait()
    into[1].wait()
    for kind, scale in enumerate((SCALE, 1.0)):
        total = sums[kind] + back[kind].astype(F32)
        out[kind] = (total.T * scale).astype(BF16)
        away[kind].start()
    for j in (2, 3):
        into[j].wait()
        away[j].start()
    for copy in away:
        copy.wait()


def solution(mesh):
    n_ctx = mesh.shape["ctx"]

    def on_device(queries, key_rows, value_rows, out_grad, doc_lengths):
        anywhere = pl.BlockSpec(memory_space=pl.ANY)
        dma = pltpu.SemaphoreType.DMA
        vmem = pltpu.VMEM
        wide = jax.ShapeDtypeStruct(queries.shape, BF16)
        narrow = jax.ShapeDtypeStruct(key_rows.shape, BF16)
        results = pl.pallas_call(
            functools.partial(kernel, n_ctx),
            out_shape=(wide, wide, jax.ShapeDtypeStruct((2, D, T), F32), jax.ShapeDtypeStruct((2, D, T), BF16)),
            in_specs=[anywhere] * 4 + [pl.BlockSpec(memory_space=pltpu.SMEM)],
            out_specs=(anywhere,) * 4,
            scratch_shapes=[
                vmem((PAIRS + 1, 2, 2 * T, D), BF16),
                vmem((ROWS, D), BF16),
                vmem((ROWS, D), BF16),
                vmem((ROWS, D), BF16),
                vmem((D, ROWS), BF16),
                vmem((D, ROWS), BF16),
                vmem((PAIRS, ROWS, 2 * T), F32),
                vmem((PAIRS, ROWS, 2 * T), BF16),
                vmem((PAIRS, ROWS, 2 * T), BF16),
                vmem((PAIRS, T, 2 * T), F32),
                vmem((ROWS, T), F32),
                vmem((ROWS, T), F32),
                vmem((ROWS, T), F32),
                vmem((ROWS, T), F32),
                vmem((ROWS, D), F32),
                vmem((ROWS, D), BF16),
                vmem((ROWS, D), BF16),
                vmem((PAIRS, 2, D, T), F32),
                vmem((PAIRS, 2, D, T), BF16),
                vmem((PAIRS, 2, D, T), BF16),
                vmem((PAIRS, 2, D, T), BF16),
                vmem((5, 2, D, T), BF16),
                vmem((5, 2, D, T), BF16),
                vmem((2, D, T), BF16),
                vmem((2, T, D), BF16),
                dma, dma, dma((2,)), dma, dma, dma,
                dma((2,)), dma((2,)), dma((2,)), dma((8,)), dma((8,)), dma((18,)), dma((18,)), dma((18,)),
                dma((13,)), dma((4,)), dma((8,)), dma((2,)),
            ],
            compiler_params=pltpu.CompilerParams(
                collective_id=0, has_side_effects=True, vmem_limit_bytes=60 * 1024 * 1024
            ),
        )(queries, key_rows, value_rows, out_grad, doc_lengths)
        return pl.pallas_call(
            finish,
            out_shape=(wide, wide, narrow, narrow),
            in_specs=[anywhere] * 4,
            out_specs=(anywhere,) * 4,
            scratch_shapes=[
                vmem(wide.shape, BF16), vmem(wide.shape, BF16), vmem((2, D, T), F32), vmem((2, D, T), BF16),
                vmem((2, T, D), BF16), dma((4,)), dma((4,)),
            ],
            compiler_params=pltpu.CompilerParams(vmem_limit_bytes=62 * 1024 * 1024),
        )(*results)

    split = P("ctx", "head")
    return jax.shard_map(
        on_device, mesh=mesh, in_specs=(split, split, split, split, P()), out_specs=(split,) * 4, check_vma=False
    )
```

```python
import functools
import math

import jax
import jax.numpy as jnp
from jax import lax
from jax.experimental import pallas as pl
from jax.experimental.pallas import tpu as pltpu
from jax.sharding import PartitionSpec as P

MESH = pl.DeviceIdType.MESH
T = 128
D = 128
G = 8
ROWS = T * G
PAIRS = 9
CHUNK = 256
NEG = -1e30
SCALE = D**-0.5
LOG2 = SCALE * math.log2(math.e)
NT = (((1,), (1,)), ((), ()))
NN = (((1,), (0,)), ((), ()))
F32, BF16 = jnp.float32, jnp.bfloat16


def dot(a, b, dims):
    return lax.dot_general(a, b, dims, preferred_element_type=F32)


def kernel(
    n_ctx,
    q_hbm, k_hbm, v_hbm, g_hbm, lengths,
    att_hbm, dq_hbm, sum_hbm, r4,
    kv, qs, gs, g2, qt, gt, sbuf, pbuf, dsb, bias, m1, m2, l1, l2, acc, att, dqo,
    part, s1, r1, s2, r2, r3, s3, transit,
    ld_q, ld_g, ld_kv, st_att, st_dq, st_kv,
    z_s, t_s, t_r, own_s, rel_s, fwd_s, kr, fr, g1_r, g2_r, g3_r, g4_r,
):
    c = lax.axis_index("ctx")
    z = lax.rem(c // 2, 2)
    core = lax.rem(c, 2)
    mate = c + 1 - 2 * core
    across = c + 2 - 4 * z

    def along_z(step):
        at = lax.rem(z * 8 + lax.axis_index("head") + step, 16)
        return {"ctx": c - 2 * z + 2 * (at // 8), "head": lax.rem(at, 8)}, at // 8

    ahead, z_ahead = along_z(4 + 8 * core)
    behind, _ = along_z(12 - 8 * core)
    low, high = pl.ds(0, T), pl.ds(T, T)

    def send(src, dst, ss, rs, dev):
        return pltpu.make_async_remote_copy(
            src_ref=src, dst_ref=dst, send_sem=ss, recv_sem=rs, device_id=dev if isinstance(dev, dict) else {"ctx": dev}, device_id_type=MESH
        )

    def whole(ref, sem):
        return pltpu.make_async_copy(ref, ref, sem)

    own_in = [
        pltpu.make_async_copy(src, kv.at[0, kind, low], ld_kv.at[kind]) for kind, src in enumerate((k_hbm, v_hbm))
    ]
    q_in = [
        pltpu.make_async_copy(q_hbm.at[:, pl.ds(h * D, D)], qs.at[pl.ds(h * T, T)], ld_q) for h in range(G)
    ]
    g_in = [
        pltpu.make_async_copy(g_hbm.at[:, pl.ds(h * D, D)], gs.at[pl.ds(h * T, T)], ld_g) for h in range(G)
    ]
    for copy in own_in:
        copy.start()

    barrier = pltpu.get_barrier_semaphore()
    for dev in ({"ctx": mate}, behind):
        pl.semaphore_signal(barrier, inc=1, device_id=dev, device_id_type=MESH)
    count = 2
    for d in range(1, 5):
        count = count + (c + 4 * d < n_ctx).astype(jnp.int32)

        @pl.when(c - 4 * d >= 0)
        def _():
            pl.semaphore_signal(barrier, inc=1, device_id={"ctx": c - 4 * d}, device_id_type=MESH)

    for copy in own_in:
        copy.wait()
    pl.semaphore_wait(barrier, count)

    land = 9 - 8 * z_ahead
    here = 9 - 8 * z

    def z_send(kind):
        return send(kv.at[0, kind, low], transit.at[kind], z_s.at[kind], t_r.at[kind], ahead)

    def z_pass(kind):
        return send(transit.at[kind], kv.at[land, kind, low], t_s.at[kind], kr.at[far(land, kind)], ahead)

    def pass_along(kind):
        z_send(kind).wait_recv()
        z_pass(kind).start()

    def own_send(d, kind):
        at = 4 * kind + d - 1
        return send(kv.at[0, kind, low], kv.at[2 * d, kind, low], own_s.at[at], kr.at[at], c + 4 * d)

    def far(i, kind):
        return 8 + 5 * kind + (i - 1) // 2

    def far_swapped(i, kind):
        return 5 + 4 * kind + (i - 1) // 2

    def relay_send(d, kind):
        to = 2 * d - 1 + 2 * z
        return send(
            kv.at[here, kind, low], kv.at[to, kind, low], rel_s.at[4 * kind + d - 1], kr.at[far(to, kind)], c + 4 * d
        )

    def near_forward(i, kind):
        at = 5 * kind + i // 2
        return send(kv.at[i, kind, low], kv.at[i, kind, high], fwd_s.at[at], fr.at[at], mate)

    def far_forward(i, kind):
        at = far_swapped(i, kind) + 5
        return send(kv.at[i, kind, low], kv.at[i, kind, high], fwd_s.at[at], fr.at[at], mate)

    def near_arrived(i, kind):
        return send(kv.at[i, kind, low], kv.at[i, kind, low], z_s.at[0], kr.at[4 * kind + i // 2 - 1], mate)

    def far_arrived(i, kind):
        return send(kv.at[i, kind, low], kv.at[i, kind, low], z_s.at[kind], kr.at[far(i, kind)], mate)

    relays = lambda d: (c + 4 * d < n_ctx) & (2 * d - 1 + 2 * z < PAIRS)

    def start_sends(kind):
        z_send(kind).start()
        for d in (2, 1, 3, 4):

            @pl.when(c + 4 * d < n_ctx)
            def _():
                own_send(d, kind).start()

        near_forward(0, kind).start()

    start_sends(0)
    for copy in q_in + g_in:
        copy.start()

    for i in range(1, PAIRS):

        @pl.when(c < 2 * i)
        def _():
            kv[i] = jnp.zeros((2, 2 * T, D), BF16)

    for d in range(1, 5):

        @pl.when(c + 4 * d >= n_ctx)
        def _():
            r2[d] = jnp.zeros((2, D, T), BF16)

        @pl.when((c + 4 * d >= n_ctx) | (2 * d - 1 + 2 * z >= PAIRS))
        def _():
            r3[d] = jnp.zeros((2, D, T), BF16)

    row = c * T + lax.broadcasted_iota(jnp.int32, (T, 2 * T), 0)
    lane = lax.broadcasted_iota(jnp.int32, (T, 2 * T), 1)
    doc = jnp.zeros((T, 2 * T), jnp.int32)
    start = jnp.int32(0)
    for j in range(lengths.shape[0]):
        doc = jnp.where(row >= start, start, doc)
        start = start + lengths[j]
    first = lane + jnp.where(lane < T, c * T, mate * T - T)

    def mask(i, _):
        key = first - i * (2 * T)
        bias[i] = jnp.where((key >= doc) & (key <= row), 0.0, NEG)
        return 0

    lax.fori_loop(0, PAIRS, mask, 0)
    whole(qs, ld_q).wait()
    m1[...] = jnp.full_like(m1, NEG)
    m2[...] = jnp.full_like(m2, NEG)
    for ref in (l1, l2, acc):
        ref[...] = jnp.zeros_like(ref)

    def scores(i, most):
        key = kv[i, 0]
        b = bias[i]
        b = jnp.concatenate([b, b], axis=0)
        for t in range(ROWS // CHUNK):
            rows = pl.ds(t * CHUNK, CHUNK)
            s = dot(qs[rows], key, NT) + b
            sbuf[i, rows] = s
            most[rows] = jnp.maximum(most[rows], jnp.maximum(s[:, :T], s[:, T:]))

    def wide(x):
        return jnp.concatenate([x, x], axis=1)

    def weigh(i, most, total):
        for t in range(ROWS // CHUNK):
            rows = pl.ds(t * CHUNK, CHUNK)
            p = jnp.exp2((sbuf[i, rows] - wide(most[rows])) * LOG2)
            total[rows] += p[:, :T] + p[:, T:]
            pbuf[i, rows] = p.astype(BF16)

    def spread(x):
        return jnp.broadcast_to(x, (x.shape[0], T))

    def take_near(i, kind):
        @pl.when(c >= 2 * i)
        def _():
            near_arrived(i, kind).wait_recv()
            near_forward(i, kind).start()

    def await_near(i, kind):
        @pl.when(c >= 2 * i)
        def _():
            near_forward(i, kind).wait_recv()

    def take_far(i, kind):
        @pl.when(c >= 2 * i)
        def _():
            far_arrived(i, kind).wait_recv()
            far_forward(i, kind).start()

    def await_far(i, kind):
        @pl.when(c >= 2 * i)
        def _():
            far_forward(i, kind).wait_recv()

    def near_pair(n):
        return jnp.where(n < 2, 2 * n, 12 - 2 * n)

    def near_scores(n, _):
        i = near_pair(n)

        @pl.when(n == 1)
        def _():
            start_sends(1)
            pass_along(0)

        @pl.when(n < 4)
        def _():
            take_near(near_pair(n + 1), 0)

        await_near(i, 0)
        scores(i, m1)
        return 0

    lax.fori_loop(0, 5, near_scores, 0)
    for h in range(G):
        rows = pl.ds(h * T, T)
        m1[rows] = spread(jnp.max(m1[rows], axis=1, keepdims=True))
        qt[:, rows] = qs[rows].T

    def near_weigh(n, _):
        i = near_pair(n)

        @pl.when(n < 4)
        def _():
            take_near(near_pair(n + 1), 1)

        @pl.when(n == 1)
        def _():
            pass_along(1)

        await_near(i, 1)
        weigh(i, m1, l1)
        for t in range(ROWS // CHUNK):
            rows = pl.ds(t * CHUNK, CHUNK)
            acc[rows] += dot(pbuf[i, rows], kv[i, 1], NN)
        return 0

    lax.fori_loop(0, 5, near_weigh, 0)
    for h in range(G):
        rows = pl.ds(h * T, T)
        l1[rows] = spread(jnp.sum(l1[rows], axis=1, keepdims=True))
    whole(gs, ld_g).wait()

    for kind in range(2):
        far_arrived(here, kind).wait_recv()
        for d in (2, 1, 3, 4):

            @pl.when(relays(d))
            def _():
                relay_send(d, kind).start()

        @pl.when(z == 1)
        def _():
            far_forward(1, kind).start()

    @pl.when(z == 0)
    def _():
        take_far(1, 0)

    def far_arrival(n):
        up = jnp.where(n == 0, 1, 9 - 2 * n)
        down = jnp.where(n == 0, 1, jnp.where(n == 1, 3, 11 - 2 * n))
        return jnp.where(z == 0, up, down)

    take_far(far_arrival(1), 0)

    def far_scores(n, _):
        i = far_arrival(n)

        @pl.when(n < 2)
        def _():
            take_far(far_arrival(n + 2), 0)

        await_far(i, 0)
        scores(i, m2)
        return 0

    lax.fori_loop(0, 4, far_scores, 0)

    @pl.when(z == 0)
    def _():
        take_far(1, 1)

    for n in (1, 2, 3):
        take_far(far_arrival(n), 1)

    for h in range(G):
        rows = pl.ds(h * T, T)
        old = m1[rows]
        most = jnp.maximum(old, spread(jnp.max(m2[rows], axis=1, keepdims=True)))
        m2[rows] = most
        m1[rows] = jnp.exp2((old - most) * LOG2)

    def far_weigh(n, _):
        weigh(2 * n + 1, m2, l2)
        return 0

    lax.fori_loop(0, 4, far_weigh, 0)
    for h in range(G):
        rows = pl.ds(h * T, T)
        inverse = 1.0 / (m1[rows] * l1[rows] + spread(jnp.sum(l2[rows], axis=1, keepdims=True)))
        l2[rows] = inverse
        grad = (gs[rows].astype(F32) * inverse).astype(BF16)
        g2[rows] = grad
        gt[:, rows] = grad.T

    def near_swap(i):
        return send(s1.at[i], r1.at[i], fwd_s.at[i // 2], g1_r.at[i // 2], mate)

    def far_swap(i, kind):
        return send(s1.at[i, kind], r1.at[i, kind], fwd_s.at[far_swapped(i, 1 - kind) + 5], g1_r.at[far_swapped(i, kind)], mate)

    def home(d):
        return send(s2.at[2 * d], r2.at[d], own_s.at[d - 1], g2_r.at[d - 1], c - 4 * d)

    def to_relay(i, kind):
        d = (i + 1) // 2 - z
        return send(
            s2.at[i, kind], r3.at[d, kind], rel_s.at[4 - 4 * kind + (i - 1) // 2], g3_r.at[4 * kind + d - 1], c - 4 * d
        )

    def back_across(kind):
        return send(s3.at[kind], r4.at[kind], z_s.at[kind], g4_r.at[kind], across)

    def gather_sent(kind):
        z_send(kind).wait_send()
        z_pass(kind).wait_send()
        for d in range(1, 5):

            @pl.when(relays(d))
            def _():
                relay_send(d, kind).wait_send()

        for i in (1, 3, 5, 7):

            @pl.when(c >= 2 * i)
            def _():
                far_forward(i, kind).wait_send()

    def near_sent():
        for d in range(1, 5):

            @pl.when(c + 4 * d < n_ctx)
            def _():
                for kind in range(2):
                    own_send(d, kind).wait_send()

        for i in range(0, PAIRS, 2):

            @pl.when(c >= 2 * i)
            def _():
                for kind in range(2):
                    near_forward(i, kind).wait_send()

    def child(d):
        return (c + 4 * d < n_ctx) & (2 * d - 1 + 2 * z < PAIRS)

    def keep(i, kind, value):
        part[i, kind] = value[:, :T]
        s1[i, kind] = value[:, T:].astype(BF16)

    def give(i, kind, value):
        keep(i, kind, value)

        @pl.when(c >= 2 * i)
        def _():
            far_swap(i, kind).start()

    def pass_far(i, kind):
        @pl.when(c >= 2 * i)
        def _():
            far_swap(i, kind).wait_recv()
            total = part[i, kind] + r1[i, kind].astype(F32)
            part[i, kind] = total
            s2[i, kind] = total.astype(BF16)

            @pl.when((z == 0) | (i > 1))
            def _():
                to_relay(i, kind).start()

    def pass_near(i):
        @pl.when(c >= 2 * i)
        def _():
            near_swap(i).wait_recv()
            s2[i] = (part[i] + r1[i].astype(F32)).astype(BF16)
            home(i // 2).start()

    def relay_back(kind):
        for d in range(1, 5):

            @pl.when(child(d))
            def _():
                send(s2.at[0, kind], r3.at[d, kind], z_s.at[kind], g3_r.at[4 * kind + d - 1], mate).wait_recv()

        total = r3[1, kind].astype(F32) + r3[2, kind].astype(F32) + r3[3, kind].astype(F32) + r3[4, kind].astype(F32)
        s3[kind] = (total + part[1, kind] * z.astype(F32)).astype(BF16)
        back_across(kind).start()

    def far_pair(n):
        up = jnp.where(n == 0, 3, jnp.where(n == 1, 5, jnp.where(n == 2, 1, 7)))
        down = jnp.where(n == 0, 5, jnp.where(n == 1, 7, jnp.where(n == 2, 3, 1)))
        return jnp.where(z == 0, up, down)

    def far_values(n, _):
        i = far_pair(n)
        give(i, 1, dot(gt[...], pbuf[i], NN))
        return 0

    gather_sent(0)
    lax.fori_loop(0, 4, far_values, 0)

    for n in range(4):
        await_far(2 * n + 1, 1)

    def attend(t, _):
        rows = pl.ds(pl.multiple_of(t * CHUNK, CHUNK), CHUNK)
        weights = jnp.concatenate([pbuf[i, rows] for i in (1, 3, 5, 7)], axis=1)
        values = jnp.concatenate([kv[i, 1] for i in (1, 3, 5, 7)], axis=0)
        total = acc[rows] * m1[rows] + dot(weights, values, NN)
        inverse = l2[rows]
        out = (total * inverse).astype(BF16)
        att[rows] = out
        delta = jnp.sum(g2[rows].astype(F32) * out.astype(F32), axis=1, keepdims=True)
        l1[rows] = spread(delta)
        return 0

    lax.fori_loop(0, ROWS // CHUNK, attend, 0)

    def pass_values(n, _):
        pass_far(far_pair(n), 1)
        return 0

    lax.fori_loop(0, 4, pass_values, 0)

    def score_grads(i, grads, deltas, after):
        value = kv[i, 1]
        for t in range(ROWS // CHUNK):
            rows = pl.ds(t * CHUNK, CHUNK)
            ds = dot(grads[rows], value, NT) - wide(deltas[rows])
            dsb[i, rows] = (pbuf[i, rows].astype(F32) * ds).astype(BF16)
        after(i, 0, dot(qt[...], dsb[i], NN))

    def far_keys(n, _):
        score_grads(far_pair(n), g2, l1, give)

        @pl.when(n > 1)
        def _():
            pass_far(far_pair(n - 2), 0)

        return 0

    gather_sent(1)
    lax.fori_loop(0, 4, far_keys, 0)
    near_sent()
    att_out = [
        pltpu.make_async_copy(att.at[pl.ds(h * T, T)], att_hbm.at[:, pl.ds(h * D, D)], st_att) for h in range(G)
    ]
    for copy in att_out:
        copy.start()
    for h in range(G):
        rows = pl.ds(h * T, T)
        grad = (gs[rows].astype(F32) * (l2[rows] * m1[rows])).astype(BF16)
        gs[rows] = grad
        gt[:, rows] = grad.T
        l1[rows] = spread(jnp.sum(grad.astype(F32) * att[rows].astype(F32), axis=1, keepdims=True))
    pass_far(far_pair(2), 0)
    pass_far(far_pair(3), 0)

    def near(n, _):
        i = 8 - 2 * n
        keep(i, 1, dot(gt[...], pbuf[i], NN))
        score_grads(i, gs, l1, keep)

        @pl.when(c >= 2 * i)
        def _():
            near_swap(i).start()

        @pl.when(n == 0)
        def _():
            relay_back(1)

        @pl.when(n > 1)
        def _():
            pass_near(i + 4)

        @pl.when(n == 2)
        def _():
            relay_back(0)

        return 0

    lax.fori_loop(0, 5, near, 0)
    pass_near(2)

    def query_grads(t, _):
        rows = pl.ds(pl.multiple_of(t * CHUNK, CHUNK), CHUNK)
        grads = jnp.concatenate([dsb[i, rows] for i in range(PAIRS)], axis=1)
        keys = jnp.concatenate([kv[i, 0] for i in range(PAIRS)], axis=0)
        total = dot(grads, keys, NN)
        dqo[rows] = (total * SCALE).astype(BF16)
        return 0

    lax.fori_loop(0, ROWS // CHUNK, query_grads, 0)
    dq_out = [
        pltpu.make_async_copy(dqo.at[pl.ds(h * T, T)], dq_hbm.at[:, pl.ds(h * D, D)], st_dq) for h in range(G)
    ]
    for copy in dq_out:
        copy.start()

    near_swap(0).wait_recv()
    for d in range(1, 5):

        @pl.when(c + 4 * d < n_ctx)
        def _():
            send(s2.at[0], r2.at[d], z_s.at[0], g2_r.at[d - 1], mate).wait_recv()

    for kind in range(2):
        total = part[0, kind] + r1[0, kind].astype(F32)
        for d in range(1, 5):
            total = total + r2[d, kind].astype(F32)
        part[0, kind] = total

    for i in range(PAIRS):

        @pl.when(c >= 2 * i)
        def _():
            if i % 2 == 0:
                near_swap(i).wait_send()
                if i > 0:
                    home(i // 2).wait_send()
            else:
                for kind in range(2):
                    far_swap(i, kind).wait_send()
                    if i > 1:
                        to_relay(i, kind).wait_send()

    @pl.when((z == 0) & (c >= 2))
    def _():
        for kind in range(2):
            to_relay(1, kind).wait_send()

    sums_out = pltpu.make_async_copy(part.at[0], sum_hbm, st_kv)
    sums_out.start()
    for copy in (whole(att, st_att), whole(dqo, st_dq), sums_out):
        copy.wait()
    for kind in range(2):
        back_across(kind).wait_send()
    for kind in (1, 0):
        back_across(kind).wait_recv()


def finish(att_in, dq_in, sums_in, back_in, att_out, dq_out, dk_out, dv_out, att, dq, sums, back, out, sem_in, sem_out):
    def copies(pairs, sems):
        return [pltpu.make_async_copy(a, b, sems.at[j]) for j, (a, b) in enumerate(pairs)]

    into = copies(((back_in, back), (sums_in, sums), (att_in, att), (dq_in, dq)), sem_in)
    away = copies(((out.at[0], dk_out), (out.at[1], dv_out), (att, att_out), (dq, dq_out)), sem_out)
    for copy in into:
        copy.start()
    into[0].wait()
    into[1].wait()
    for kind, scale in enumerate((SCALE, 1.0)):
        total = sums[kind] + back[kind].astype(F32)
        out[kind] = (total.T * scale).astype(BF16)
        away[kind].start()
    for j in (2, 3):
        into[j].wait()
        away[j].start()
    for copy in away:
        copy.wait()


def solution(mesh):
    n_ctx = mesh.shape["ctx"]

    def on_device(queries, key_rows, value_rows, out_grad, doc_lengths):
        anywhere = pl.BlockSpec(memory_space=pl.ANY)
        dma = pltpu.SemaphoreType.DMA
        vmem = pltpu.VMEM
        wide = jax.ShapeDtypeStruct(queries.shape, BF16)
        narrow = jax.ShapeDtypeStruct(key_rows.shape, BF16)
        results = pl.pallas_call(
            functools.partial(kernel, n_ctx),
            out_shape=(wide, wide, jax.ShapeDtypeStruct((2, D, T), F32), jax.ShapeDtypeStruct((2, D, T), BF16)),
            in_specs=[anywhere] * 4 + [pl.BlockSpec(memory_space=pltpu.SMEM)],
            out_specs=(anywhere,) * 4,
            scratch_shapes=[
                vmem((PAIRS + 1, 2, 2 * T, D), BF16),
                vmem((ROWS, D), BF16),
                vmem((ROWS, D), BF16),
                vmem((ROWS, D), BF16),
                vmem((D, ROWS), BF16),
                vmem((D, ROWS), BF16),
                vmem((PAIRS, ROWS, 2 * T), F32),
                vmem((PAIRS, ROWS, 2 * T), BF16),
                vmem((PAIRS, ROWS, 2 * T), BF16),
                vmem((PAIRS, T, 2 * T), F32),
                vmem((ROWS, T), F32),
                vmem((ROWS, T), F32),
                vmem((ROWS, T), F32),
                vmem((ROWS, T), F32),
                vmem((ROWS, D), F32),
                vmem((ROWS, D), BF16),
                vmem((ROWS, D), BF16),
                vmem((PAIRS, 2, D, T), F32),
                vmem((PAIRS, 2, D, T), BF16),
                vmem((PAIRS, 2, D, T), BF16),
                vmem((PAIRS, 2, D, T), BF16),
                vmem((5, 2, D, T), BF16),
                vmem((5, 2, D, T), BF16),
                vmem((2, D, T), BF16),
                vmem((2, T, D), BF16),
                dma, dma, dma((2,)), dma, dma, dma,
                dma((2,)), dma((2,)), dma((2,)), dma((8,)), dma((8,)), dma((18,)), dma((18,)), dma((18,)),
                dma((13,)), dma((4,)), dma((8,)), dma((2,)),
            ],
            compiler_params=pltpu.CompilerParams(
                collective_id=0, has_side_effects=True, vmem_limit_bytes=60 * 1024 * 1024
            ),
        )(queries, key_rows, value_rows, out_grad, doc_lengths)
        return pl.pallas_call(
            finish,
            out_shape=(wide, wide, narrow, narrow),
            in_specs=[anywhere] * 4,
            out_specs=(anywhere,) * 4,
            scratch_shapes=[
                vmem(wide.shape, BF16), vmem(wide.shape, BF16), vmem((2, D, T), F32), vmem((2, D, T), BF16),
                vmem((2, T, D), BF16), dma((4,)), dma((4,)),
            ],
            compiler_params=pltpu.CompilerParams(vmem_limit_bytes=62 * 1024 * 1024),
        )(*results)

    split = P("ctx", "head")
    return jax.shard_map(
        on_device, mesh=mesh, in_specs=(split, split, split, split, P()), out_specs=(split,) * 4, check_vma=False
    )
```

```python
import functools
import math

import jax
import jax.numpy as jnp
from jax import lax
from jax.experimental import pallas as pl
from jax.experimental.pallas import tpu as pltpu
from jax.sharding import PartitionSpec as P

MESH = pl.DeviceIdType.MESH
T = 128
D = 128
G = 8
ROWS = T * G
PAIRS = 9
CHUNK = 256
NEG = -1e30
SCALE = D**-0.5
LOG2 = SCALE * math.log2(math.e)
NT = (((1,), (1,)), ((), ()))
NN = (((1,), (0,)), ((), ()))
F32, BF16 = jnp.float32, jnp.bfloat16


def dot(a, b, dims):
    return lax.dot_general(a, b, dims, preferred_element_type=F32)


def kernel(
    n_ctx,
    q_hbm, k_hbm, v_hbm, g_hbm, lengths,
    att_hbm, dq_hbm, sum_hbm, r4,
    kv, qs, gs, g2, qt, gt, sbuf, pbuf, dsb, bias, m1, m2, l1, l2, acc, att, dqo,
    part, s1, r1, s2, r2, r3, s3, transit,
    ld_q, ld_g, ld_kv, st_att, st_dq, st_kv,
    z_s, t_s, t_r, own_s, rel_s, fwd_s, kr, fr, g1_r, g2_r, g3_r, g4_r,
):
    c = lax.axis_index("ctx")
    z = lax.rem(c // 2, 2)
    core = lax.rem(c, 2)
    mate = c + 1 - 2 * core
    across = c + 2 - 4 * z

    def along_z(step):
        at = lax.rem(z * 8 + lax.axis_index("head") + step, 16)
        return {"ctx": c - 2 * z + 2 * (at // 8), "head": lax.rem(at, 8)}, at // 8

    ahead, z_ahead = along_z(4 + 8 * core)
    behind, _ = along_z(12 - 8 * core)
    low, high = pl.ds(0, T), pl.ds(T, T)

    def send(src, dst, ss, rs, dev):
        return pltpu.make_async_remote_copy(
            src_ref=src, dst_ref=dst, send_sem=ss, recv_sem=rs, device_id=dev if isinstance(dev, dict) else {"ctx": dev}, device_id_type=MESH
        )

    def whole(ref, sem):
        return pltpu.make_async_copy(ref, ref, sem)

    own_in = [
        pltpu.make_async_copy(src, kv.at[0, kind, low], ld_kv.at[kind]) for kind, src in enumerate((k_hbm, v_hbm))
    ]
    q_in = [
        pltpu.make_async_copy(q_hbm.at[:, pl.ds(h * D, D)], qs.at[pl.ds(h * T, T)], ld_q) for h in range(G)
    ]
    g_in = [
        pltpu.make_async_copy(g_hbm.at[:, pl.ds(h * D, D)], gs.at[pl.ds(h * T, T)], ld_g) for h in range(G)
    ]
    for copy in own_in:
        copy.start()

    barrier = pltpu.get_barrier_semaphore()
    for dev in ({"ctx": mate}, behind):
        pl.semaphore_signal(barrier, inc=1, device_id=dev, device_id_type=MESH)
    count = 2
    for d in range(1, 5):
        count = count + (c + 4 * d < n_ctx).astype(jnp.int32)

        @pl.when(c - 4 * d >= 0)
        def _():
            pl.semaphore_signal(barrier, inc=1, device_id={"ctx": c - 4 * d}, device_id_type=MESH)

    for copy in own_in:
        copy.wait()
    pl.semaphore_wait(barrier, count)

    land = 9 - 8 * z_ahead
    here = 9 - 8 * z

    def z_send(kind):
        return send(kv.at[0, kind, low], transit.at[kind], z_s.at[kind], t_r.at[kind], ahead)

    def z_pass(kind):
        return send(transit.at[kind], kv.at[land, kind, low], t_s.at[kind], kr.at[far(land, kind)], ahead)

    def pass_along(kind):
        z_send(kind).wait_recv()
        z_pass(kind).start()

    def own_send(d, kind):
        at = 4 * kind + d - 1
        return send(kv.at[0, kind, low], kv.at[2 * d, kind, low], own_s.at[at], kr.at[at], c + 4 * d)

    def far(i, kind):
        return 8 + 5 * kind + (i - 1) // 2

    def far_swapped(i, kind):
        return 5 + 4 * kind + (i - 1) // 2

    def relay_send(d, kind):
        to = 2 * d - 1 + 2 * z
        return send(
            kv.at[here, kind, low], kv.at[to, kind, low], rel_s.at[4 * kind + d - 1], kr.at[far(to, kind)], c + 4 * d
        )

    def near_forward(i, kind):
        at = 5 * kind + i // 2
        return send(kv.at[i, kind, low], kv.at[i, kind, high], fwd_s.at[at], fr.at[at], mate)

    def far_forward(i, kind):
        at = far_swapped(i, kind) + 5
        return send(kv.at[i, kind, low], kv.at[i, kind, high], fwd_s.at[at], fr.at[at], mate)

    def near_arrived(i, kind):
        return send(kv.at[i, kind, low], kv.at[i, kind, low], z_s.at[0], kr.at[4 * kind + i // 2 - 1], mate)

    def far_arrived(i, kind):
        return send(kv.at[i, kind, low], kv.at[i, kind, low], z_s.at[kind], kr.at[far(i, kind)], mate)

    relays = lambda d: (c + 4 * d < n_ctx) & (2 * d - 1 + 2 * z < PAIRS)

    def start_sends(kind):
        z_send(kind).start()
        for d in (2, 1, 3, 4):

            @pl.when(c + 4 * d < n_ctx)
            def _():
                own_send(d, kind).start()

        near_forward(0, kind).start()

    start_sends(0)
    for copy in q_in + g_in:
        copy.start()

    for i in range(1, PAIRS):

        @pl.when(c < 2 * i)
        def _():
            kv[i] = jnp.zeros((2, 2 * T, D), BF16)

    for d in range(1, 5):

        @pl.when(c + 4 * d >= n_ctx)
        def _():
            r2[d] = jnp.zeros((2, D, T), BF16)

        @pl.when((c + 4 * d >= n_ctx) | (2 * d - 1 + 2 * z >= PAIRS))
        def _():
            r3[d] = jnp.zeros((2, D, T), BF16)

    row = c * T + lax.broadcasted_iota(jnp.int32, (T, 2 * T), 0)
    lane = lax.broadcasted_iota(jnp.int32, (T, 2 * T), 1)
    doc = jnp.zeros((T, 2 * T), jnp.int32)
    start = jnp.int32(0)
    for j in range(lengths.shape[0]):
        doc = jnp.where(row >= start, start, doc)
        start = start + lengths[j]
    first = lane + jnp.where(lane < T, c * T, mate * T - T)

    def mask(i, _):
        key = first - i * (2 * T)
        bias[i] = jnp.where((key >= doc) & (key <= row), 0.0, NEG)
        return 0

    lax.fori_loop(0, PAIRS, mask, 0)
    whole(qs, ld_q).wait()
    m1[...] = jnp.full_like(m1, NEG)
    m2[...] = jnp.full_like(m2, NEG)
    for ref in (l1, l2, acc):
        ref[...] = jnp.zeros_like(ref)

    def scores(i, most):
        key = kv[i, 0]
        b = bias[i]
        b = jnp.concatenate([b, b], axis=0)
        for t in range(ROWS // CHUNK):
            rows = pl.ds(t * CHUNK, CHUNK)
            s = dot(qs[rows], key, NT) + b
            sbuf[i, rows] = s
            most[rows] = jnp.maximum(most[rows], jnp.maximum(s[:, :T], s[:, T:]))

    def wide(x):
        return jnp.concatenate([x, x], axis=1)

    def weigh(i, most, total):
        for t in range(ROWS // CHUNK):
            rows = pl.ds(t * CHUNK, CHUNK)
            p = jnp.exp2((sbuf[i, rows] - wide(most[rows])) * LOG2)
            total[rows] += p[:, :T] + p[:, T:]
            pbuf[i, rows] = p.astype(BF16)

    def spread(x):
        return jnp.broadcast_to(x, (x.shape[0], T))

    def take_near(i, kind):
        @pl.when(c >= 2 * i)
        def _():
            near_arrived(i, kind).wait_recv()
            near_forward(i, kind).start()

    def await_near(i, kind):
        @pl.when(c >= 2 * i)
        def _():
            near_forward(i, kind).wait_recv()

    def take_far(i, kind):
        @pl.when(c >= 2 * i)
        def _():
            far_arrived(i, kind).wait_recv()
            far_forward(i, kind).start()

    def await_far(i, kind):
        @pl.when(c >= 2 * i)
        def _():
            far_forward(i, kind).wait_recv()

    def near_pair(n):
        return jnp.where(n < 2, 2 * n, 12 - 2 * n)

    def near_scores(n, _):
        i = near_pair(n)

        @pl.when(n == 1)
        def _():
            start_sends(1)
            pass_along(0)

        @pl.when(n < 4)
        def _():
            take_near(near_pair(n + 1), 0)

        await_near(i, 0)
        scores(i, m1)
        return 0

    lax.fori_loop(0, 5, near_scores, 0)
    for h in range(G):
        rows = pl.ds(h * T, T)
        m1[rows] = spread(jnp.max(m1[rows], axis=1, keepdims=True))
        qt[:, rows] = qs[rows].T

    def near_weigh(n, _):
        i = near_pair(n)

        @pl.when(n < 4)
        def _():
            take_near(near_pair(n + 1), 1)

        @pl.when(n == 1)
        def _():
            pass_along(1)

        await_near(i, 1)
        weigh(i, m1, l1)
        for t in range(ROWS // CHUNK):
            rows = pl.ds(t * CHUNK, CHUNK)
            acc[rows] += dot(pbuf[i, rows], kv[i, 1], NN)
        return 0

    lax.fori_loop(0, 5, near_weigh, 0)
    for h in range(G):
        rows = pl.ds(h * T, T)
        l1[rows] = spread(jnp.sum(l1[rows], axis=1, keepdims=True))
    whole(gs, ld_g).wait()

    for kind in range(2):
        far_arrived(here, kind).wait_recv()
        for d in (2, 1, 3, 4):

            @pl.when(relays(d))
            def _():
                relay_send(d, kind).start()

        @pl.when(z == 1)
        def _():
            far_forward(1, kind).start()

    @pl.when(z == 0)
    def _():
        take_far(1, 0)

    def far_arrival(n):
        up = jnp.where(n == 0, 1, 9 - 2 * n)
        down = jnp.where(n == 0, 1, jnp.where(n == 1, 3, 11 - 2 * n))
        return jnp.where(z == 0, up, down)

    take_far(far_arrival(1), 0)

    def far_scores(n, _):
        i = far_arrival(n)

        @pl.when(n < 2)
        def _():
            take_far(far_arrival(n + 2), 0)

        await_far(i, 0)
        scores(i, m2)
        return 0

    lax.fori_loop(0, 4, far_scores, 0)

    @pl.when(z == 0)
    def _():
        take_far(1, 1)

    for n in (1, 2, 3):
        take_far(far_arrival(n), 1)

    for h in range(G):
        rows = pl.ds(h * T, T)
        old = m1[rows]
        most = jnp.maximum(old, spread(jnp.max(m2[rows], axis=1, keepdims=True)))
        m2[rows] = most
        m1[rows] = jnp.exp2((old - most) * LOG2)

    def far_weigh(n, _):
        weigh(2 * n + 1, m2, l2)
        return 0

    lax.fori_loop(0, 4, far_weigh, 0)
    for h in range(G):
        rows = pl.ds(h * T, T)
        inverse = 1.0 / (m1[rows] * l1[rows] + spread(jnp.sum(l2[rows], axis=1, keepdims=True)))
        l2[rows] = inverse
        grad = (gs[rows].astype(F32) * inverse).astype(BF16)
        g2[rows] = grad
        gt[:, rows] = grad.T

    def near_swap(i):
        return send(s1.at[i], r1.at[i], fwd_s.at[i // 2], g1_r.at[i // 2], mate)

    def far_swap(i, kind):
        return send(s1.at[i, kind], r1.at[i, kind], fwd_s.at[far_swapped(i, 1 - kind) + 5], g1_r.at[far_swapped(i, kind)], mate)

    def home(d):
        return send(s2.at[2 * d], r2.at[d], own_s.at[d - 1], g2_r.at[d - 1], c - 4 * d)

    def to_relay(i, kind):
        d = (i + 1) // 2 - z
        return send(
            s2.at[i, kind], r3.at[d, kind], rel_s.at[4 - 4 * kind + (i - 1) // 2], g3_r.at[4 * kind + d - 1], c - 4 * d
        )

    def back_across(kind):
        return send(s3.at[kind], r4.at[kind], z_s.at[kind], g4_r.at[kind], across)

    def gather_sent(kind):
        z_send(kind).wait_send()
        z_pass(kind).wait_send()
        for d in range(1, 5):

            @pl.when(relays(d))
            def _():
                relay_send(d, kind).wait_send()

        for i in (1, 3, 5, 7):

            @pl.when(c >= 2 * i)
            def _():
                far_forward(i, kind).wait_send()

    def near_sent():
        for d in range(1, 5):

            @pl.when(c + 4 * d < n_ctx)
            def _():
                for kind in range(2):
                    own_send(d, kind).wait_send()

        for i in range(0, PAIRS, 2):

            @pl.when(c >= 2 * i)
            def _():
                for kind in range(2):
                    near_forward(i, kind).wait_send()

    def child(d):
        return (c + 4 * d < n_ctx) & (2 * d - 1 + 2 * z < PAIRS)

    def keep(i, kind, value):
        part[i, kind] = value[:, :T]
        s1[i, kind] = value[:, T:].astype(BF16)

    def give(i, kind, value):
        keep(i, kind, value)

        @pl.when(c >= 2 * i)
        def _():
            far_swap(i, kind).start()

    def pass_far(i, kind):
        @pl.when(c >= 2 * i)
        def _():
            far_swap(i, kind).wait_recv()
            total = part[i, kind] + r1[i, kind].astype(F32)
            part[i, kind] = total
            s2[i, kind] = total.astype(BF16)

            @pl.when((z == 0) | (i > 1))
            def _():
                to_relay(i, kind).start()

    def pass_near(i):
        @pl.when(c >= 2 * i)
        def _():
            near_swap(i).wait_recv()
            s2[i] = (part[i] + r1[i].astype(F32)).astype(BF16)
            home(i // 2).start()

    def relay_back(kind):
        for d in range(1, 5):

            @pl.when(child(d))
            def _():
                send(s2.at[0, kind], r3.at[d, kind], z_s.at[kind], g3_r.at[4 * kind + d - 1], mate).wait_recv()

        total = r3[1, kind].astype(F32) + r3[2, kind].astype(F32) + r3[3, kind].astype(F32) + r3[4, kind].astype(F32)
        s3[kind] = (total + part[1, kind] * z.astype(F32)).astype(BF16)
        back_across(kind).start()

    def far_pair(n):
        up = jnp.where(n == 0, 3, jnp.where(n == 1, 5, jnp.where(n == 2, 1, 7)))
        down = jnp.where(n == 0, 5, jnp.where(n == 1, 7, jnp.where(n == 2, 3, 1)))
        return jnp.where(z == 0, up, down)

    def far_values(n, _):
        i = far_pair(n)
        give(i, 1, dot(gt[...], pbuf[i], NN))
        return 0

    gather_sent(0)
    lax.fori_loop(0, 4, far_values, 0)

    for n in range(4):
        await_far(2 * n + 1, 1)

    def attend(t, _):
        rows = pl.ds(pl.multiple_of(t * CHUNK, CHUNK), CHUNK)
        weights = jnp.concatenate([pbuf[i, rows] for i in (1, 3, 5, 7)], axis=1)
        values = jnp.concatenate([kv[i, 1] for i in (1, 3, 5, 7)], axis=0)
        total = acc[rows] * m1[rows] + dot(weights, values, NN)
        inverse = l2[rows]
        out = (total * inverse).astype(BF16)
        att[rows] = out
        delta = jnp.sum(g2[rows].astype(F32) * out.astype(F32), axis=1, keepdims=True)
        l1[rows] = spread(delta)
        return 0

    lax.fori_loop(0, ROWS // CHUNK, attend, 0)

    def pass_values(n, _):
        pass_far(far_pair(n), 1)
        return 0

    lax.fori_loop(0, 4, pass_values, 0)

    def score_grads(i, grads, deltas, after):
        value = kv[i, 1]
        for t in range(ROWS // CHUNK):
            rows = pl.ds(t * CHUNK, CHUNK)
            ds = dot(grads[rows], value, NT) - wide(deltas[rows])
            dsb[i, rows] = (pbuf[i, rows].astype(F32) * ds).astype(BF16)
        after(i, 0, dot(qt[...], dsb[i], NN))

    def far_keys(n, _):
        score_grads(far_pair(n), g2, l1, give)

        @pl.when(n > 1)
        def _():
            pass_far(far_pair(n - 2), 0)

        return 0

    gather_sent(1)
    lax.fori_loop(0, 4, far_keys, 0)
    near_sent()
    att_out = [
        pltpu.make_async_copy(att.at[pl.ds(h * T, T)], att_hbm.at[:, pl.ds(h * D, D)], st_att) for h in range(G)
    ]
    for copy in att_out:
        copy.start()
    for h in range(G):
        rows = pl.ds(h * T, T)
        grad = (gs[rows].astype(F32) * (l2[rows] * m1[rows])).astype(BF16)
        gs[rows] = grad
        gt[:, rows] = grad.T
        l1[rows] = spread(jnp.sum(grad.astype(F32) * att[rows].astype(F32), axis=1, keepdims=True))
    pass_far(far_pair(2), 0)
    pass_far(far_pair(3), 0)

    def near_order(n):
        return jnp.where(n < 3, 4 + 2 * n, 8 - 2 * n)

    def near(n, _):
        i = near_order(n)
        keep(i, 1, dot(gt[...], pbuf[i], NN))
        score_grads(i, gs, l1, keep)

        @pl.when(c >= 2 * i)
        def _():
            near_swap(i).start()

        @pl.when(n == 0)
        def _():
            relay_back(1)

        @pl.when(n > 1)
        def _():
            pass_near(near_order(n - 2))

        @pl.when(n == 2)
        def _():
            relay_back(0)

        return 0

    lax.fori_loop(0, 5, near, 0)
    pass_near(2)

    def query_grads(t, _):
        rows = pl.ds(pl.multiple_of(t * CHUNK, CHUNK), CHUNK)
        grads = jnp.concatenate([dsb[i, rows] for i in range(PAIRS)], axis=1)
        keys = jnp.concatenate([kv[i, 0] for i in range(PAIRS)], axis=0)
        total = dot(grads, keys, NN)
        dqo[rows] = (total * SCALE).astype(BF16)
        return 0

    lax.fori_loop(0, ROWS // CHUNK, query_grads, 0)
    dq_out = [
        pltpu.make_async_copy(dqo.at[pl.ds(h * T, T)], dq_hbm.at[:, pl.ds(h * D, D)], st_dq) for h in range(G)
    ]
    for copy in dq_out:
        copy.start()

    near_swap(0).wait_recv()
    for d in range(1, 5):

        @pl.when(c + 4 * d < n_ctx)
        def _():
            send(s2.at[0], r2.at[d], z_s.at[0], g2_r.at[d - 1], mate).wait_recv()

    for kind in range(2):
        total = part[0, kind] + r1[0, kind].astype(F32)
        for d in range(1, 5):
            total = total + r2[d, kind].astype(F32)
        part[0, kind] = total

    for i in range(PAIRS):

        @pl.when(c >= 2 * i)
        def _():
            if i % 2 == 0:
                near_swap(i).wait_send()
                if i > 0:
                    home(i // 2).wait_send()
            else:
                for kind in range(2):
                    far_swap(i, kind).wait_send()
                    if i > 1:
                        to_relay(i, kind).wait_send()

    @pl.when((z == 0) & (c >= 2))
    def _():
        for kind in range(2):
            to_relay(1, kind).wait_send()

    sums_out = pltpu.make_async_copy(part.at[0], sum_hbm, st_kv)
    sums_out.start()
    for copy in (whole(att, st_att), whole(dqo, st_dq), sums_out):
        copy.wait()
    for kind in range(2):
        back_across(kind).wait_send()
    for kind in (1, 0):
        back_across(kind).wait_recv()


def finish(att_in, dq_in, sums_in, back_in, att_out, dq_out, dk_out, dv_out, att, dq, sums, back, out, sem_in, sem_out):
    def copies(pairs, sems):
        return [pltpu.make_async_copy(a, b, sems.at[j]) for j, (a, b) in enumerate(pairs)]

    into = copies(((back_in, back), (sums_in, sums), (att_in, att), (dq_in, dq)), sem_in)
    away = copies(((out.at[0], dk_out), (out.at[1], dv_out), (att, att_out), (dq, dq_out)), sem_out)
    for copy in into:
        copy.start()
    into[0].wait()
    into[1].wait()
    for kind, scale in enumerate((SCALE, 1.0)):
        total = sums[kind] + back[kind].astype(F32)
        out[kind] = (total.T * scale).astype(BF16)
        away[kind].start()
    for j in (2, 3):
        into[j].wait()
        away[j].start()
    for copy in away:
        copy.wait()


def solution(mesh):
    n_ctx = mesh.shape["ctx"]

    def on_device(queries, key_rows, value_rows, out_grad, doc_lengths):
        anywhere = pl.BlockSpec(memory_space=pl.ANY)
        dma = pltpu.SemaphoreType.DMA
        vmem = pltpu.VMEM
        wide = jax.ShapeDtypeStruct(queries.shape, BF16)
        narrow = jax.ShapeDtypeStruct(key_rows.shape, BF16)
        results = pl.pallas_call(
            functools.partial(kernel, n_ctx),
            out_shape=(wide, wide, jax.ShapeDtypeStruct((2, D, T), F32), jax.ShapeDtypeStruct((2, D, T), BF16)),
            in_specs=[anywhere] * 4 + [pl.BlockSpec(memory_space=pltpu.SMEM)],
            out_specs=(anywhere,) * 4,
            scratch_shapes=[
                vmem((PAIRS + 1, 2, 2 * T, D), BF16),
                vmem((ROWS, D), BF16),
                vmem((ROWS, D), BF16),
                vmem((ROWS, D), BF16),
                vmem((D, ROWS), BF16),
                vmem((D, ROWS), BF16),
                vmem((PAIRS, ROWS, 2 * T), F32),
                vmem((PAIRS, ROWS, 2 * T), BF16),
                vmem((PAIRS, ROWS, 2 * T), BF16),
                vmem((PAIRS, T, 2 * T), F32),
                vmem((ROWS, T), F32),
                vmem((ROWS, T), F32),
                vmem((ROWS, T), F32),
                vmem((ROWS, T), F32),
                vmem((ROWS, D), F32),
                vmem((ROWS, D), BF16),
                vmem((ROWS, D), BF16),
                vmem((PAIRS, 2, D, T), F32),
                vmem((PAIRS, 2, D, T), BF16),
                vmem((PAIRS, 2, D, T), BF16),
                vmem((PAIRS, 2, D, T), BF16),
                vmem((5, 2, D, T), BF16),
                vmem((5, 2, D, T), BF16),
                vmem((2, D, T), BF16),
                vmem((2, T, D), BF16),
                dma, dma, dma((2,)), dma, dma, dma,
                dma((2,)), dma((2,)), dma((2,)), dma((8,)), dma((8,)), dma((18,)), dma((18,)), dma((18,)),
                dma((13,)), dma((4,)), dma((8,)), dma((2,)),
            ],
            compiler_params=pltpu.CompilerParams(
                collective_id=0, has_side_effects=True, vmem_limit_bytes=60 * 1024 * 1024
            ),
        )(queries, key_rows, value_rows, out_grad, doc_lengths)
        return pl.pallas_call(
            finish,
            out_shape=(wide, wide, narrow, narrow),
            in_specs=[anywhere] * 4,
            out_specs=(anywhere,) * 4,
            scratch_shapes=[
                vmem(wide.shape, BF16), vmem(wide.shape, BF16), vmem((2, D, T), F32), vmem((2, D, T), BF16),
                vmem((2, T, D), BF16), dma((4,)), dma((4,)),
            ],
            compiler_params=pltpu.CompilerParams(vmem_limit_bytes=62 * 1024 * 1024),
        )(*results)

    split = P("ctx", "head")
    return jax.shard_map(
        on_device, mesh=mesh, in_specs=(split, split, split, split, P()), out_specs=(split,) * 4, check_vma=False
    )
```
